512 devices in a mesh: pages: 16 (over y, core), row: 8 (over z), col: 4 (over x).
Axes of the slice: x: 4, y: 8, z: 8, core: 2. Of those that a mesh axis runs over, the one named last changes fastest.
Arguments:
- residual: bfloat16 [512, 2, 2048], P('pages', None, ('row', 'col')), may hold values from -6 to 6
- fresh_qkv: bfloat16 [512, 2, 3, 2048], P('pages', None, None, 'col'), may hold values from -27 to 27
- prefix_pages: bfloat16 [256, 2, 128, 2048], P('pages', None, 'row', 'col'), may hold values from -6 to 6
- tail_pages: bfloat16 [512, 2, 128, 2048], P('pages', None, 'row', 'col'), may hold values from -6 to 6
- prefix_item: int32 [256], replicated, may hold values from 0 to 255, as said below
- tail_item: int32 [512], replicated, may hold values from 0 to 511, as said below
- prefix_length: int32 [32], replicated, may hold values from 1 to 1024, 20480 in all
- tail_length: int32 [512], replicated, may hold values from 1 to 128, 40960 in all
- out_weight: bfloat16 [2048, 2048], P('col', 'row'), may hold values from -0.125 to 0.125
- out_bias: bfloat16 [2048], P(('row', 'col')), may hold values from -4 to 4
- mlp_gain: bfloat16 [2048], P('row'), may hold values from 0.25 to 1.75
- mlp_shift: bfloat16 [2048], P('row'), may hold values from -4 to 4
- up_weight: bfloat16 [2048, 8192], P('row', 'col'), may hold values from -0.125 to 0.125
- up_bias: bfloat16 [8192], P(('col', 'row')), may hold values from -4 to 4
- down_weight: bfloat16 [8192, 2048], P('col', 'row'), may hold values from -0.0625 to 0.0625
- down_bias: bfloat16 [2048], P(('row', 'col')), may hold values from -4 to 4
- next_gain: bfloat16 [2048], P('row'), may hold values from 0.25 to 1.75
- next_shift: bfloat16 [2048], P('row'), may hold values from -4 to 4
- score_weight: bfloat16 [2048], P('row'), may hold values from -0.125 to 0.125
- qkv_weight: bfloat16 [2048, 6144], P('row', 'col'), may hold values from -0.125 to 0.125
- qkv_bias: bfloat16 [6144], P(('col', 'row')), may hold values from -4 to 4
Outputs:
- layer_out: bfloat16 [512, 2, 2048], P('pages', None, ('row', 'col'))
- score_out: float32 [512, 2], P('pages')
- projected_next: bfloat16 [512, 2, 6144], P('pages', None, ('col', 'row'))
The draws below stay inside these ranges and needn't reach their ends.
Inputs may be any that keep to these rules, and one draw needn't show every extreme that they name: `prefix_item`: each of the 256 prompt pages is held by exactly one slot; slot h * 16 + g + k (k < 1) holds a page of one of the prompts g * 2 to (g + 1) * 2 - 1. `tail_item`: each continuation's tail is held by exactly one slot; slot h * 32 + g * 2 + k (k < 2) holds the tail of one of the continuations g * 32 to (g + 1) * 32 - 1. `prefix_length`: some prompt has exactly 1024 cached tokens. `tail_length`: some continuation has exactly 128 tail tokens.
All inputs are finite; a program needn't handle non-finite values.
Results may differ from the reference program's by a relative error of at most 0.023.
Values may be sent and summed in bfloat16 or wider, within the bound.
No kernel may reach another device: no remote copies, remote signals or barrier semaphores. Data moves between devices by JAX's collectives and lax.ppermute only.
A program may use at most 64 MiB of HBM per device.

```python
import math
import jax
import jax.numpy as jnp
import numpy as np
from jax import lax

D = 2048
H = 16
HD = 128
FF = 8192
PAGE = 128
MAXPAGES = 8
CONT = 16
GROUPS = 16
PROMPTS = 32
BATCH_GRP = 32
BATCH = 512
PSLOTS = 16
PAIR_PAGES = 1
PAIR_TAILS = 2


def spread_items(base_key, per_group, groups_total, pair_count):
    orders = jax.vmap(lambda group_id: jax.random.permutation(jax.random.fold_in(base_key, group_id), per_group))(jnp.arange(groups_total, dtype=jnp.int32))
    item_table = orders.astype(jnp.int32) + (jnp.arange(groups_total, dtype=jnp.int32) * per_group)[:, None]
    return item_table.reshape(groups_total, groups_total, pair_count).transpose(1, 0, 2).reshape(-1)


def draw_prefix_item(key, part):
    return spread_items(jax.random.fold_in(key, 7), PSLOTS, GROUPS, PAIR_PAGES)


def draw_tail_item(key, part):
    return spread_items(jax.random.fold_in(key, 11), BATCH_GRP, GROUPS, PAIR_TAILS)


def draw_fresh_qkv(key, part):
    full_shape = (BATCH, 2, 3, D)
    return jnp.clip(jax.random.normal(key, full_shape, jnp.float32), -6.0, 6.0).astype(jnp.bfloat16)


def block_scale(key, extent, shards, smallest, high):
    factor_of = 1.0
    for axis_at, parts in shards:
        draws = jax.random.uniform(jax.random.fold_in(jax.random.fold_in(key, 6), axis_at), (parts,), jnp.float32, smallest / len(shards), high / len(shards))
        factor_of = factor_of * jnp.repeat(jnp.exp(draws), extent[axis_at] // parts).reshape((-1,) + (1,) * (len(extent) - 1 - axis_at))
    return factor_of


def split_up(number_of, total, limit, skew):
    weights = [(1 << 20) // math.isqrt(standing ** skew) + 1 for standing in range(2, number_of + 1)]
    rest, given = total - limit - (number_of - 1), [1] * (number_of - 1)
    while rest > 0:
        candidates = [i for i in range(number_of - 1) if given[i] < limit]
        pool, left = sum([weights[i] for i in candidates]), rest
        for i in candidates:
            more = min(limit - given[i], max(1, left * weights[i] // pool), rest)
            given[i] = given[i] + more
            rest = rest - more
    return np.array([limit] + given)


def uneven(rng, count, total, most, skew):
    if count == 2:
        one = jax.random.randint(rng, (), max(1, total - most), min(most, total - 1) + 1)
        return jnp.stack([one, total - one])
    lengths = jnp.asarray(split_up(count, total, most, skew), jnp.int32)
    twos = (count - 1) // 2
    giver, taker = lengths[1:1 + 2 * twos:2], lengths[2:2 + 2 * twos:2]
    slack = jnp.minimum(giver - 1, most - taker)
    passed = jax.random.randint(jax.random.fold_in(rng, 1), (twos,), 0, 1 << 20) % (slack + 1)
    lengths = lengths.at[1:1 + 2 * twos:2].set(giver - passed).at[2:2 + 2 * twos:2].set(taker + passed)
    return lengths[jax.random.permutation(jax.random.fold_in(rng, 2), count)]


def gaussian(rng, dims, scale, most, pieces=(), kind=jnp.bfloat16):
    factor_of = block_scale(rng, dims, pieces, -0.22, 0.18) if pieces else 1.0
    values = jax.random.normal(rng, dims, jnp.float32) * scale * factor_of
    return jnp.minimum(jnp.maximum(values, -most), most).astype(kind)


def setup_inputs(seed: int = 0) -> dict:
    splits = jax.random.split(jax.random.key(seed), 22)
    return {
        "residual": gaussian(splits[0], (BATCH, 2, D), 1.0, 6.0, ((0, 16), (2, 32))),
        "fresh_qkv": draw_fresh_qkv(jax.random.fold_in(splits[21], 71), 0),
        "prefix_pages": gaussian(splits[2], (PROMPTS * MAXPAGES, 2, PAGE, D), 1.0, 6.0, ((0, 16), (2, 8), (3, 4))),
        "tail_pages": gaussian(splits[3], (BATCH, 2, PAGE, D), 1.0, 6.0, ((0, 16), (2, 8), (3, 4))),
        "prefix_item": draw_prefix_item(jax.random.fold_in(splits[21], 71), 0),
        "tail_item": draw_tail_item(jax.random.fold_in(splits[21], 71), 0),
        "prefix_length": uneven(splits[6], PROMPTS, PROMPTS * MAXPAGES * PAGE * 5 // 8, MAXPAGES * PAGE, 1).astype(jnp.int32),
        "tail_length": uneven(splits[7], BATCH, BATCH * PAGE * 5 // 8, PAGE, 1).astype(jnp.int32),
        "out_weight": gaussian(splits[8], (D, D), D ** -0.5, 0.125, ((0, 4), (1, 8))),
        "out_bias": gaussian(splits[9], (D,), 0.3, 4.0, ((0, 32),)),
        "mlp_gain": jnp.clip(1.0 + 0.15 * jax.random.normal(splits[10], (D,), jnp.float32), 0.25, 1.75).astype(jnp.bfloat16),
        "mlp_shift": gaussian(splits[11], (D,), 0.3, 4.0, ((0, 8),)),
        "up_weight": gaussian(splits[12], (D, FF), D ** -0.5, 0.125, ((0, 8), (1, 4))),
        "up_bias": gaussian(splits[13], (FF,), 0.5, 4.0, ((0, 32),)),
        "down_weight": gaussian(splits[14], (FF, D), FF ** -0.5, 0.0625, ((0, 4), (1, 8))),
        "down_bias": gaussian(splits[15], (D,), 0.3, 4.0, ((0, 32),)),
        "next_gain": jnp.clip(1.0 + 0.15 * jax.random.normal(splits[16], (D,), jnp.float32), 0.25, 1.75).astype(jnp.bfloat16),
        "next_shift": gaussian(splits[17], (D,), 0.3, 4.0, ((0, 8),)),
        "score_weight": gaussian(splits[18], (D,), D ** -0.5, 0.125, ((0, 8),)),
        "qkv_weight": gaussian(splits[19], (D, 3 * D), D ** -0.5, 0.125, ((0, 8), (1, 4))),
        "qkv_bias": gaussian(splits[20], (3 * D,), 0.3, 4.0, ((0, 32),)),
    }


masked_score = -1e+30
norm_eps = 1e-05

def layer_norm(values, gain, shift):
    center = lax.optimization_barrier(jnp.mean(values, axis=-1, keepdims=True))
    spread = lax.optimization_barrier(jnp.mean(values * values, axis=-1, keepdims=True)) - center * center
    return (values - center) * lax.rsqrt(spread + norm_eps) * gain.astype(jnp.float32) + shift.astype(jnp.float32)

def reference(residual, fresh_qkv, prefix_pages, tail_pages, prefix_item, tail_item, prefix_length, tail_length, out_weight, out_bias, mlp_gain, mlp_shift, up_weight, up_bias, down_weight, down_bias, next_gain, next_shift, score_weight, qkv_weight, qkv_bias):
    highest = lax.Precision.HIGHEST
    page_slot = jnp.zeros((PROMPTS * MAXPAGES,), jnp.int32).at[prefix_item].set(jnp.arange(PROMPTS * MAXPAGES, dtype=jnp.int32))
    tail_slot = jnp.zeros((BATCH,), jnp.int32).at[tail_item].set(jnp.arange(BATCH, dtype=jnp.int32))
    head_index = jnp.arange(H, dtype=jnp.int32)
    slopes = jnp.exp2(-8.0 * (head_index + 1).astype(jnp.float32) / H)
    span_one = MAXPAGES * PAGE

    def one_prompt(prompt):
        page_rows = page_slot[prompt * MAXPAGES + jnp.arange(MAXPAGES, dtype=jnp.int32)]
        cached = prefix_pages[page_rows].astype(jnp.float32)
        prefix_keys = cached[:, 0].reshape(span_one, H, HD)
        prefix_values = cached[:, 1].reshape(span_one, H, HD)
        members = prompt * CONT + jnp.arange(CONT, dtype=jnp.int32)
        tail_rows = tail_pages[tail_slot[members]].astype(jnp.float32)
        tail_keys = tail_rows[:, 0].reshape(CONT, PAGE, H, HD)
        tail_values = tail_rows[:, 1].reshape(CONT, PAGE, H, HD)
        fresh_rows = fresh_qkv[members].astype(jnp.float32).reshape(CONT, 2, 3, H, HD)
        queries = fresh_rows[:, :, 0]
        prompt_len = prefix_length[prompt]
        tail_lens = tail_length[members]
        step_index = jnp.arange(2, dtype=jnp.int32)
        query_pos = prompt_len + tail_lens[:, None] + step_index[None, :]
        prefix_pos = jnp.arange(span_one, dtype=jnp.int32)
        tail_pos = jnp.arange(PAGE, dtype=jnp.int32)
        slope_grid = slopes[None, None, :, None]
        prefix_scores = jnp.einsum('cuhd,khd->cuhk', queries, prefix_keys, precision=highest) / math.sqrt(HD)
        prefix_scores = prefix_scores + slope_grid * (prefix_pos[None, None, None, :] - query_pos[:, :, None, None]).astype(jnp.float32)
        prefix_usable = jnp.broadcast_to((prefix_pos < prompt_len)[None, None, None, :], prefix_scores.shape)
        tail_scores = jnp.einsum('cuhd,cjhd->cuhj', queries, tail_keys, precision=highest) / math.sqrt(HD)
        tail_scores = tail_scores + slope_grid * (tail_pos[None, None, None, :] - tail_lens[:, None, None, None] - step_index[None, :, None, None]).astype(jnp.float32)
        tail_usable = jnp.broadcast_to((tail_pos[None, :] < tail_lens[:, None])[:, None, None, :], tail_scores.shape)
        new_scores = jnp.einsum('cuhd,cvhd->cuhv', queries, fresh_rows[:, :, 1], precision=highest) / math.sqrt(HD)
        new_scores = new_scores + slope_grid * (step_index[None, None, None, :] - step_index[None, :, None, None]).astype(jnp.float32)
        new_usable = jnp.broadcast_to((step_index[None, :] <= step_index[:, None])[None, :, None, :], new_scores.shape)
        scores = jnp.concatenate([prefix_scores, tail_scores, new_scores], axis=3)
        usable = jnp.concatenate([prefix_usable, tail_usable, new_usable], axis=3)
        scores = jnp.where(usable, scores, masked_score)
        row_max = lax.optimization_barrier(jnp.max(scores, axis=3, keepdims=True))
        weights = jnp.where(usable, jnp.exp(scores - row_max), 0.0)
        weight_sum = lax.optimization_barrier(jnp.sum(weights, axis=3))
        outputs = jnp.einsum('cuhk,khd->cuhd', weights[..., :span_one], prefix_values, precision=highest)
        outputs = outputs + jnp.einsum('cuhj,cjhd->cuhd', weights[..., span_one:span_one + PAGE], tail_values, precision=highest)
        outputs = outputs + jnp.einsum('cuhv,cvhd->cuhd', weights[..., span_one + PAGE:], fresh_rows[:, :, 2], precision=highest)
        return (outputs / weight_sum[..., None]).reshape(CONT, 2, D).astype(jnp.bfloat16)
    attended = lax.map(one_prompt, jnp.arange(PROMPTS, dtype=jnp.int32)).reshape(BATCH * 2, D)
    hidden_one = residual.reshape(BATCH * 2, D).astype(jnp.float32) + jnp.dot(attended, out_weight, preferred_element_type=jnp.float32) + out_bias.astype(jnp.float32)
    normed_a = layer_norm(hidden_one, mlp_gain, mlp_shift).astype(jnp.bfloat16)
    hidden_two = jax.nn.gelu(jnp.dot(normed_a, up_weight, preferred_element_type=jnp.float32) + up_bias.astype(jnp.float32), approximate=True).astype(jnp.bfloat16)
    layer_out = (hidden_one + jnp.dot(hidden_two, down_weight, preferred_element_type=jnp.float32) + down_bias.astype(jnp.float32)).astype(jnp.bfloat16)
    out_wide = layer_out.astype(jnp.float32)
    score_out = lax.optimization_barrier(jnp.sum(out_wide * score_weight.astype(jnp.float32), axis=1))
    normed_b = layer_norm(out_wide, next_gain, next_shift).astype(jnp.bfloat16)
    projected_next = (jnp.dot(normed_b, qkv_weight, preferred_element_type=jnp.float32) + qkv_bias.astype(jnp.float32)).astype(jnp.bfloat16)
    return (layer_out.reshape(BATCH, 2, D), score_out.reshape(BATCH, 2), projected_next.reshape(BATCH, 2, 3 * D))
```

```python
import math

import jax
import jax.numpy as jnp
from jax import lax
from jax.experimental import pallas as pl
from jax.experimental.pallas import tpu as pltpu
from jax.sharding import PartitionSpec as P

D = 2048
H = 16
HD = 128
PAGE = 128
MAXPAGES = 8
CONT = 16

GROUPS = 16
NROW = 8
NCOL = 4
ROWS = 64
HEADS = 4
WIDE = HEADS * HD
PACK = WIDE + 128
BLOCK = D // NROW
TOK = 16
TAILS = 32

masked_score = -1e30
norm_eps = 1e-05
f32 = jnp.float32
bf16 = jnp.bfloat16


def dot(a, b):
    return jnp.dot(a, b, preferred_element_type=f32)


def dot_t(a, b):
    return lax.dot_general(a, b, (((1,), (1,)), ((), ())), preferred_element_type=f32)


def iota(shape, dim):
    return lax.broadcasted_iota(jnp.int32, shape, dim)


def one_hot(mask):
    return jnp.where(mask, 1.0, 0.0).astype(bf16)


def rounded(x):
    return x.astype(bf16).astype(f32)


def slope_of(head):
    return jnp.exp2(jnp.full((ROWS, 1), -8.0 / H, f32) * (head + 1).astype(f32))


def put_stats(stats, head, m, l):
    lane = iota((ROWS, 128), 1)
    hi = rounded(l)
    stats = jnp.where(lane == head * 4, m, stats)
    stats = jnp.where(lane == head * 4 + 1, hi, stats)
    return jnp.where(lane == head * 4 + 2, l - hi, stats)


def get_stats(stats, head):
    at = head * 4
    return stats[:, at : at + 1], stats[:, at + 1 : at + 2] + stats[:, at + 2 : at + 3]


def send_kernel(tail_item, query, pages, out):
    group = lax.axis_index("pages")
    row = iota((ROWS, ROWS), 0)
    source = jnp.zeros((ROWS, ROWS), jnp.int32)
    for j in range(TAILS):
        item = tail_item[(j // 2) * TAILS + group * 2 + j % 2] - group * TAILS
        source = jnp.where((row >> 1) == j, item * 2, source)
    pick = one_hot(iota((ROWS, ROWS), 1) == source + (row & 1))
    picked = dot(pick, query[...])
    for h in range(GROUPS):
        out[h, 0:TOK] = pages[h, 0]
        out[h, TOK : 2 * TOK] = pages[h, 1]
        out[h, 2 * TOK : 2 * TOK + 4] = picked[4 * h : 4 * h + 4].astype(bf16)


def tail_kernel(tail_item, tail_length, recv, tails, out, wide):
    holder = lax.axis_index("pages")
    token_at = lax.axis_index("row") * TOK
    first_head = lax.axis_index("col") * HEADS
    for g in range(GROUPS):
        wide[4 * g : 4 * g + 4, 0:WIDE] = recv[g, 2 * TOK : 2 * TOK + 4].astype(f32)
    row = iota((ROWS, 1), 0)
    lens = jnp.zeros((ROWS, 1), jnp.int32)
    for s in range(TAILS):
        lens = jnp.where((row >> 1) == s, tail_length[tail_item[holder * TAILS + s]], lens)
    keys = TAILS * TOK
    key = iota((ROWS, keys), 1)
    token = (key & (TOK - 1)) + token_at
    usable = ((key >> 4) == (row >> 1)) & (token < lens)
    offset = (token - lens - (row & 1)).astype(f32)
    stats = jnp.zeros((ROWS, 128), f32)
    for head in range(HEADS):
        at = slice(head * HD, (head + 1) * HD)
        k = tails[:, 0, :, at].reshape(keys, HD)
        v = tails[:, 1, :, at].reshape(keys, HD)
        scores = dot_t(wide[:, at].astype(bf16), k) * (1.0 / math.sqrt(HD))
        scores = scores + slope_of(first_head + head) * offset
        scores = jnp.where(usable, scores, masked_score)
        m = rounded(jnp.max(scores, axis=1, keepdims=True))
        weights = jnp.where(usable, jnp.exp(scores - m), 0.0)
        stats = put_stats(stats, head, m, jnp.sum(weights, axis=1, keepdims=True))
        wide[:, at] = dot(weights.astype(bf16), v)
    wide[:, WIDE:PACK] = stats
    for g in range(GROUPS):
        out[g] = wide[4 * g : 4 * g + 4].astype(bf16)


def prefix_kernel(prefix_item, prefix_length, tail_length, fresh, recv, out):
    group = lax.axis_index("pages")
    row_index = lax.axis_index("row")
    first_head = lax.axis_index("col") * HEADS
    row = iota((ROWS, 1), 0)
    tail_lens = jnp.zeros((ROWS, 1), jnp.int32)
    for j in range(TAILS):
        tail_lens = jnp.where((row >> 1) == j, tail_length[group * TAILS + j], tail_lens)
    row_prompt = row >> 5
    prompt_lens = jnp.where(
        row_prompt == 0, prefix_length[group * 2], prefix_length[group * 2 + 1]
    )
    query_pos = prompt_lens + tail_lens + (row & 1)
    keys = GROUPS * TOK
    lane = iota((1, keys), 1)
    key_pos = (lane & (TOK - 1)) + row_index * TOK
    key_prompt = jnp.zeros((1, keys), jnp.int32)
    for h in range(GROUPS):
        item = prefix_item[h * GROUPS + group]
        here = (lane >> 4) == h
        key_pos = key_pos + jnp.where(here, (item & (MAXPAGES - 1)) * PAGE, 0)
        key_prompt = jnp.where(here, (item >> 3) - group * 2, key_prompt)
    usable = (key_prompt == row_prompt) & (key_pos < prompt_lens)
    offset = (key_pos - query_pos).astype(f32)
    col = iota((ROWS, ROWS), 1)
    new_usable = ((col >> 1) == (row >> 1)) & ((col & 1) <= (row & 1)) & (row_index == 0)
    new_offset = ((col & 1) - (row & 1)).astype(f32)
    stats = jnp.zeros((ROWS, 128), f32)
    for head in range(HEADS):
        at = slice(head * HD, (head + 1) * HD)
        q = fresh[:, head * HD : (head + 1) * HD]
        new_k = fresh[:, WIDE + head * HD : WIDE + (head + 1) * HD]
        new_v = fresh[:, 2 * WIDE + head * HD : 2 * WIDE + (head + 1) * HD]
        k = recv[:, 0:TOK, at].reshape(keys, HD)
        v = recv[:, TOK : 2 * TOK, at].reshape(keys, HD)
        slope = slope_of(first_head + head)
        scores = dot_t(q, k) * (1.0 / math.sqrt(HD)) + slope * offset
        scores = jnp.where(usable, scores, masked_score)
        new_scores = dot_t(q, new_k) * (1.0 / math.sqrt(HD)) + slope * new_offset
        new_scores = jnp.where(new_usable, new_scores, masked_score)
        m = rounded(
            jnp.maximum(
                jnp.max(scores, axis=1, keepdims=True),
                jnp.max(new_scores, axis=1, keepdims=True),
            )
        )
        weights = jnp.where(usable, jnp.exp(scores - m), 0.0)
        new_weights = jnp.where(new_usable, jnp.exp(new_scores - m), 0.0)
        total = jnp.sum(weights, axis=1, keepdims=True) + jnp.sum(
            new_weights, axis=1, keepdims=True
        )
        stats = put_stats(stats, head, m, total)
        out[:, at] = dot(weights.astype(bf16), v) + dot(new_weights.astype(bf16), new_v)
    out[:, WIDE:PACK] = stats


def join_kernel(tail_item, prefix, recv, out, wide):
    group = lax.axis_index("pages")
    for h in range(GROUPS):
        wide[4 * h : 4 * h + 4] = recv[h].astype(f32)
    lane = iota((1, ROWS), 1)
    target = lane & 1
    for j in range(TAILS):
        item = tail_item[(j // 2) * TAILS + group * 2 + j % 2] - group * TAILS
        target = target + jnp.where((lane >> 1) == j, item * 2, 0)
    order = one_hot(iota((ROWS, ROWS), 0) == target)
    tails = dot(order, wide[...].astype(bf16))
    tail_stats = tails[:, WIDE:PACK]
    prefix_stats = prefix[:, WIDE:PACK]
    stats = jnp.zeros((ROWS, 128), f32)
    for head in range(HEADS):
        at = slice(head * HD, (head + 1) * HD)
        left_m, left_l = get_stats(prefix_stats, head)
        right_m, right_l = get_stats(tail_stats, head)
        m = jnp.maximum(left_m, right_m)
        left = jnp.exp(left_m - m)
        right = jnp.exp(right_m - m)
        stats = put_stats(stats, head, m, left * left_l + right * right_l)
        joined = (left * prefix[:, at] + right * tails[:, at]).astype(bf16)
        for n in range(NROW):
            out[n, :, at] = joined
    stats = stats.astype(bf16)
    for n in range(NROW):
        out[n, :, WIDE:PACK] = stats


def own_columns():
    share = BLOCK // NCOL
    first = lax.axis_index("col") * share
    return one_hot(iota((share, BLOCK), 1) == iota((share, BLOCK), 0) + first)


def out_kernel(recv, weight, residual, bias, out, wide):
    stats = [recv[n, :, WIDE:PACK].astype(f32) for n in range(NROW)]
    for head in range(HEADS):
        at = slice(head * HD, (head + 1) * HD)
        parts = [get_stats(s, head) for s in stats]
        m = parts[0][0]
        for part in parts[1:]:
            m = jnp.maximum(m, part[0])
        total = jnp.zeros((ROWS, 1), f32)
        attended = jnp.zeros((ROWS, HD), f32)
        for n in range(NROW):
            scale = jnp.exp(parts[n][0] - m)
            total = total + scale * parts[n][1]
            attended = attended + scale * recv[n, :, at].astype(f32)
        wide[:, at] = (attended / total).astype(bf16)
    place = own_columns()
    share = BLOCK // NCOL
    partial = (
        dot(wide[...], weight[...])
        + dot(residual[...], place)
        + dot(jnp.broadcast_to(bias[...], (8, share)), place)[0:1]
    ).astype(bf16)
    for n in range(NCOL):
        out[n] = partial


def split(x):
    hi = rounded(x)
    return hi, x - hi


def centred(values, gain):
    mean = jnp.mean(values, axis=1, keepdims=True)
    away = values - mean
    return mean, jnp.sum(away * away, axis=1, keepdims=True), (away * gain).astype(bf16)


def as_rows(columns):
    lane = iota((ROWS, 8), 1)
    table = jnp.zeros((ROWS, 8), f32)
    for at, column in columns:
        table = jnp.where(lane == at, column, table)
    eye = one_hot(iota((ROWS, ROWS), 0) == iota((ROWS, ROWS), 1))
    return lax.dot_general(
        table.astype(bf16), eye, (((0,), (0,)), ((), ())), preferred_element_type=f32
    )


def gain_rows(gain, shift):
    row = iota((16, BLOCK), 0)
    gain = jnp.broadcast_to(gain.astype(f32), (16, BLOCK))
    shift = jnp.broadcast_to(shift.astype(f32), (16, BLOCK))
    return jnp.where(row == 0, gain, jnp.where(row == 1, shift, 0.0)).astype(bf16)


def up_kernel(recv, gain, shift, weight, hidden, out):
    values = recv[0].astype(f32)
    for n in range(1, NCOL):
        values = values + recv[n].astype(f32)
    hidden[...] = values
    mean, spread, scaled = centred(values, gain[...].astype(f32))
    columns = list(zip((4, 5, 6, 7), split(mean) + split(spread)))
    rows = as_rows(columns)
    extra = gain_rows(gain[...], shift[...])
    edge = iota((8, BLOCK), 0)
    for n in range(NROW):
        w = weight[:, n * BLOCK : (n + 1) * BLOCK]
        out[n, 0:ROWS] = dot(scaled, w).astype(bf16)
        both = dot(extra, w)
        tail = jnp.zeros((8, BLOCK), f32)
        for at, row in enumerate(split(both[0:1]) + split(both[1:2])):
            tail = jnp.where(edge == at, row, tail)
        wide = jnp.concatenate([rows, jnp.zeros((8, BLOCK - ROWS), f32)], axis=1)
        out[n, ROWS : ROWS + 8] = jnp.where(edge < 4, tail, wide).astype(bf16)


def as_columns(recv):
    rows = jnp.concatenate([recv[n, ROWS : ROWS + 8, 0:ROWS].astype(f32) for n in range(NROW)], 0)
    eye = one_hot(iota((ROWS, ROWS), 0) == iota((ROWS, ROWS), 1))
    return dot_t(eye, rows.astype(bf16))


def scale_of(means, spreads):
    mean = sum(means) / NROW
    spread = sum(spreads)
    for part in means:
        spread = spread + BLOCK * (part - mean) * (part - mean)
    return mean, lax.rsqrt(spread / D + norm_eps)


def projected(recv, width, bias, gain_at, shift_at, mean_at, spread_at):
    columns = as_columns(recv)

    def column(n, at):
        return columns[:, 8 * n + at : 8 * n + at + 1] + columns[:, 8 * n + at + 1 : 8 * n + at + 2]

    means = [column(n, mean_at) for n in range(NROW)]
    mean, scale = scale_of(means, [column(n, spread_at) for n in range(NROW)])
    total = jnp.zeros((ROWS, width), f32)
    shifted = bias.astype(f32)
    for n in range(NROW):
        edge = recv[n, ROWS : ROWS + 8].astype(f32)
        gained = sum(edge[at : at + 1] for at in gain_at)
        shifted = shifted + sum(edge[at : at + 1] for at in shift_at)
        total = total + recv[n, 0:ROWS].astype(f32) + (means[n] - mean) * gained
    return total * scale + shifted


def hidden_kernel(recv, bias, out):
    v = projected(recv, BLOCK, bias[...], (0, 1), (2, 3), 4, 6)
    v = 0.5 * v * (1.0 + jnp.tanh(math.sqrt(2.0 / math.pi) * (v + 0.044715 * (v * v * v))))
    v = v.astype(bf16)
    for n in range(NROW):
        out[n] = v


def down_kernel(recv, weight, bias, out):
    share = BLOCK // NCOL
    total = dot(jnp.broadcast_to(bias[...], (8, share)), own_columns())[0:1]
    for n in range(NROW):
        total = total + dot(recv[n], weight[n * BLOCK : (n + 1) * BLOCK])
    total = total.astype(bf16)
    for n in range(NCOL):
        out[n] = total


def next_kernel(recv, hidden, gain, shift, score, weight, layer_out, out):
    values = hidden[...]
    for n in range(NCOL):
        values = values + recv[n].astype(f32)
    low = values.astype(bf16)
    values = low.astype(f32)
    layer_out[...] = dot_t(low, own_columns()).astype(bf16)
    mean, spread, scaled = centred(values, gain[...].astype(f32))
    scores = jnp.sum(values * score[...].astype(f32), axis=1, keepdims=True)
    columns = list(zip((2, 3, 4, 5, 6, 7), split(mean) + split(spread) + split(scores)))
    rows = as_rows(columns)
    extra = gain_rows(gain[...], shift[...])
    width = out.shape[2]
    edge = iota((8, width), 0)
    for n in range(NROW):
        w = weight[:, n * width : (n + 1) * width]
        out[n, 0:ROWS] = dot(scaled, w).astype(bf16)
        both = dot(extra, w)
        wide = jnp.concatenate([rows, jnp.zeros((8, width - ROWS), f32)], axis=1)
        tail = jnp.where(edge == 0, both[0:1], jnp.where(edge == 1, both[1:2], wide))
        out[n, ROWS : ROWS + 8] = tail.astype(bf16)


def final_kernel(recv, bias, projected_next, score_out):
    width = projected_next.shape[1]
    projected_next[...] = projected(recv, width, bias[...], (0,), (1,), 2, 4).astype(bf16)
    total = jnp.zeros((1, ROWS), f32)
    for n in range(NROW):
        edge = recv[n, ROWS : ROWS + 8, 0:ROWS].astype(f32)
        total = total + edge[6:7] + edge[7:8]
    score_out[...] = total


def call(kernel, out, scalars, arrays, scratch=(), flops=0):
    many = isinstance(out, list)
    outs = out if many else [out]
    moved = sum(a.size * a.dtype.itemsize for a in arrays)
    moved += sum(math.prod(s) * jnp.dtype(t).itemsize for s, t in outs)
    shapes = [jax.ShapeDtypeStruct(s, t) for s, t in outs]
    vmem = pl.BlockSpec(memory_space=pltpu.VMEM)
    return pl.pallas_call(
        kernel,
        out_shape=shapes if many else shapes[0],
        in_specs=[pl.BlockSpec(memory_space=pltpu.SMEM)] * len(scalars) + [vmem] * len(arrays),
        out_specs=[vmem] * len(outs) if many else vmem,
        scratch_shapes=[pltpu.VMEM(s, t) for s, t in scratch],
        cost_estimate=pl.CostEstimate(flops=flops, bytes_accessed=moved, transcendentals=0),
        compiler_params=pltpu.CompilerParams(vmem_limit_bytes=24 * 1024 * 1024),
        name=kernel.__name__,
    )(*scalars, *arrays)


def exchange(x, axis):
    return lax.all_to_all(x, axis, split_axis=0, concat_axis=0, tiled=True)


def shards(
    residual,
    fresh_qkv,
    prefix_pages,
    tail_pages,
    prefix_item,
    tail_item,
    prefix_length,
    tail_length,
    out_weight,
    out_bias,
    mlp_gain,
    mlp_shift,
    up_weight,
    up_bias,
    down_weight,
    down_bias,
    next_gain,
    next_shift,
    score_weight,
    qkv_weight,
    qkv_bias,
):
    cont_local = residual.shape[0]
    share = residual.shape[2]
    width = qkv_bias.shape[0]

    def line(x):
        return x.reshape(1, x.shape[0])

    fresh = fresh_qkv.reshape(ROWS, 3 * WIDE)
    query = fresh_qkv[:, :, 0].reshape(ROWS, WIDE)
    sent = call(send_kernel, ((GROUPS, 2 * TOK + 4, WIDE), bf16), [tail_item], [query, prefix_pages])
    arrived = exchange(sent, "pages")
    tails = call(
        tail_kernel,
        ((GROUPS, 4, PACK), bf16),
        [tail_item, tail_length],
        [arrived, tail_pages],
        [((ROWS, PACK), f32)],
    )
    tails = exchange(tails, "pages")
    prefix = call(
        prefix_kernel,
        ((ROWS, PACK), f32),
        [prefix_item, prefix_length, tail_length],
        [fresh, arrived],
    )
    joined = call(
        join_kernel,
        ((NROW, ROWS, PACK), bf16),
        [tail_item],
        [prefix, tails],
        [((ROWS, PACK), f32)],
    )
    joined = exchange(joined, "row")
    partial = call(
        out_kernel,
        ((NCOL, ROWS, BLOCK), bf16),
        [],
        [joined, out_weight, residual.reshape(ROWS, share), line(out_bias)],
        [((ROWS, WIDE), bf16)],
    )
    partial = exchange(partial, "col")
    hidden_one, partial = call(
        up_kernel,
        [((ROWS, BLOCK), f32), ((NROW, ROWS + 8, BLOCK), bf16)],
        [],
        [partial, line(mlp_gain), line(mlp_shift), up_weight],
    )
    partial = exchange(partial, "row")
    hidden_two = call(hidden_kernel, ((NROW, ROWS, BLOCK), bf16), [], [partial, line(up_bias)])
    hidden_two = exchange(hidden_two, "row")
    partial = call(
        down_kernel, ((NCOL, ROWS, BLOCK), bf16), [], [hidden_two, down_weight, line(down_bias)]
    )
    partial = exchange(partial, "col")
    layer_out, partial = call(
        next_kernel,
        [((ROWS, share), bf16), ((NROW, ROWS + 8, width), bf16)],
        [],
        [partial, hidden_one, line(next_gain), line(next_shift), line(score_weight), qkv_weight],
    )
    partial = exchange(partial, "row")
    projected_next, score_sum = call(
        final_kernel, [((ROWS, width), bf16), ((1, ROWS), f32)], [], [partial, line(qkv_bias)]
    )
    return (
        layer_out.reshape(cont_local, 2, share),
        score_sum.reshape(cont_local, 2),
        projected_next.reshape(cont_local, 2, width),
    )


def solution(mesh):
    in_specs = (
        P("pages", None, ("row", "col")),
        P("pages", None, None, "col"),
        P("pages", None, "row", "col"),
        P("pages", None, "row", "col"),
        P(),
        P(),
        P(),
        P(),
        P("col", "row"),
        P(("row", "col")),
        P("row"),
        P("row"),
        P("row", "col"),
        P(("col", "row")),
        P("col", "row"),
        P(("row", "col")),
        P("row"),
        P("row"),
        P("row"),
        P("row", "col"),
        P(("col", "row")),
    )
    out_specs = (
        P("pages", None, ("row", "col")),
        P("pages", None),
        P("pages", None, ("col", "row")),
    )
    return jax.shard_map(shards, mesh=mesh, in_specs=in_specs, out_specs=out_specs, check_vma=False)
```

```python
import math

import jax
import jax.numpy as jnp
from jax import lax
from jax.experimental import pallas as pl
from jax.experimental.pallas import tpu as pltpu
from jax.sharding import PartitionSpec as P

D = 2048
H = 16
HD = 128
PAGE = 128
MAXPAGES = 8
CONT = 16

GROUPS = 16
NROW = 8
NCOL = 4
ROWS = 64
HEADS = 4
WIDE = HEADS * HD
PACK = WIDE + 128
BLOCK = D // NROW
TOK = 16
TAILS = 32

masked_score = -1e30
norm_eps = 1e-05
f32 = jnp.float32
bf16 = jnp.bfloat16


def dot(a, b):
    return jnp.dot(a, b, preferred_element_type=f32)


def dot_t(a, b):
    return lax.dot_general(a, b, (((1,), (1,)), ((), ())), preferred_element_type=f32)


def iota(shape, dim):
    return lax.broadcasted_iota(jnp.int32, shape, dim)


def one_hot(mask):
    return jnp.where(mask, 1.0, 0.0).astype(bf16)


def rounded(x):
    return x.astype(bf16).astype(f32)


def slope_of(head):
    return jnp.exp2(jnp.full((ROWS, 1), -8.0 / H, f32) * (head + 1).astype(f32))


def put_stats(stats, head, m, l):
    lane = iota((ROWS, 128), 1)
    hi = rounded(l)
    stats = jnp.where(lane == head * 4, m, stats)
    stats = jnp.where(lane == head * 4 + 1, hi, stats)
    return jnp.where(lane == head * 4 + 2, l - hi, stats)


def get_stats(stats, head):
    at = head * 4
    return stats[:, at : at + 1], stats[:, at + 1 : at + 2] + stats[:, at + 2 : at + 3]


def send_kernel(tail_item, fresh, pages, out, items, query, wide, sems):
    copies = [
        pltpu.make_async_copy(tail_item, items, sems.at[0]),
        pltpu.make_async_copy(fresh.at[:, 0], query, sems.at[1]),
        pltpu.make_async_copy(pages, out.at[:, 0 : 2 * TOK], sems.at[2]),
    ]
    for copy in copies:
        copy.start()
    group = lax.axis_index("pages")
    row = iota((ROWS, ROWS), 0)
    copies[0].wait()
    source = jnp.zeros((ROWS, ROWS), jnp.int32)
    for j in range(TAILS):
        item = items[(j // 2) * TAILS + group * 2 + j % 2] - group * TAILS
        source = jnp.where((row >> 1) == j, item * 2, source)
    pick = one_hot(iota((ROWS, ROWS), 1) == source + (row & 1))
    copies[1].wait()
    for j in range(TAILS):
        wide[2 * j : 2 * j + 2] = query[j].astype(f32)
    picked = dot(pick, wide[...].astype(bf16))
    for h in range(GROUPS):
        out[h, 2 * TOK : 2 * TOK + 4] = picked[4 * h : 4 * h + 4].astype(bf16)
    copies[2].wait()


def tail_kernel(tail_item, tail_length, recv, tails, out, wide):
    holder = lax.axis_index("pages")
    token_at = lax.axis_index("row") * TOK
    first_head = lax.axis_index("col") * HEADS
    for g in range(GROUPS):
        wide[4 * g : 4 * g + 4, 0:WIDE] = recv[g, 2 * TOK : 2 * TOK + 4].astype(f32)
    row = iota((ROWS, 1), 0)
    lens = jnp.zeros((ROWS, 1), jnp.int32)
    for s in range(TAILS):
        lens = jnp.where((row >> 1) == s, tail_length[tail_item[holder * TAILS + s]], lens)
    some, keys = 16, 128
    key = iota((ROWS, keys), 1)
    token = (key & (TOK - 1)) + token_at
    usable = ((key >> 4) == ((row >> 1) & 7)) & (token < lens)
    offset = (token - lens - (row & 1)).astype(f32)
    stats = jnp.zeros((ROWS, 128), f32)
    for head in range(HEADS):
        at = slice(head * HD, (head + 1) * HD)
        q = wide[:, at].astype(bf16)
        scores = jnp.concatenate(
            [
                dot_t(q[n * some : (n + 1) * some], tails[8 * n : 8 * n + 8, 0, :, at].reshape(keys, HD))
                for n in range(ROWS // some)
            ],
            axis=0,
        ) * (1.0 / math.sqrt(HD))
        scores = scores + slope_of(first_head + head) * offset
        scores = jnp.where(usable, scores, masked_score)
        m = rounded(jnp.max(scores, axis=1, keepdims=True))
        weights = jnp.where(usable, jnp.exp(scores - m), 0.0)
        stats = put_stats(stats, head, m, jnp.sum(weights, axis=1, keepdims=True))
        weights = weights.astype(bf16)
        for n in range(ROWS // some):
            v = tails[8 * n : 8 * n + 8, 1, :, at].reshape(keys, HD)
            wide[n * some : (n + 1) * some, at] = dot(weights[n * some : (n + 1) * some], v)
    wide[:, WIDE:PACK] = stats
    for g in range(GROUPS):
        out[g] = wide[4 * g : 4 * g + 4].astype(bf16)


def own_columns():
    share = BLOCK // NCOL
    first = lax.axis_index("col") * share
    return one_hot(iota((share, BLOCK), 1) == iota((share, BLOCK), 0) + first)


def gain_rows(gain, shift):
    row = iota((16, BLOCK), 0)
    return jnp.where(row == 0, gain, jnp.where(row == 1, shift, 0.0)).astype(bf16)


def split(x):
    hi = rounded(x)
    return hi, x - hi


def prefix_kernel(
    prefix_item,
    prefix_length,
    tail_length,
    fresh,
    recv,
    residual,
    small,
    up_weight,
    qkv_weight,
    out,
    base,
    vectors,
    up_rows,
    qkv_rows,
):
    table = small[...].astype(f32)

    def line(at):
        return jnp.concatenate([table[at : at + 1], table[at + 1 : at + 2]], axis=1)

    share = BLOCK // NCOL
    place = own_columns()

    def placed(row):
        return dot(jnp.broadcast_to(row, (8, share)).astype(bf16), place)[0:1]

    base[...] = dot(residual[...], place) + placed(table[13:14, 64:128])
    rows = [line(0), line(4), line(8), placed(table[14:15, 0:64]), line(10), line(12)]
    edge = iota((8, BLOCK), 0)
    filled = jnp.zeros((8, BLOCK), f32)
    for at, values in enumerate(rows):
        filled = jnp.where(edge == at, values, filled)
    vectors[...] = filled
    both = gain_rows(line(0), line(2))
    for n in range(NROW):
        parts = dot(both, up_weight[:, n * BLOCK : (n + 1) * BLOCK])
        rows = jnp.zeros((8, BLOCK), f32)
        for at, values in enumerate(split(parts[0:1]) + split(parts[1:2])):
            rows = jnp.where(edge == at, values, rows)
        up_rows[n] = rows
    both = gain_rows(line(4), line(6))
    width = qkv_rows.shape[2]
    for n in range(NROW):
        qkv_rows[n] = dot(both, qkv_weight[:, n * width : (n + 1) * width])[0:8]
    group = lax.axis_index("pages")
    row_index = lax.axis_index("row")
    first_head = lax.axis_index("col") * HEADS
    row = iota((ROWS, 1), 0)
    tail_lens = jnp.zeros((ROWS, 1), jnp.int32)
    for j in range(TAILS):
        tail_lens = jnp.where((row >> 1) == j, tail_length[group * TAILS + j], tail_lens)
    row_prompt = row >> 5
    prompt_lens = jnp.where(
        row_prompt == 0, prefix_length[group * 2], prefix_length[group * 2 + 1]
    )
    query_pos = prompt_lens + tail_lens + (row & 1)
    keys = GROUPS * TOK
    lane = iota((1, keys), 1)
    key_pos = (lane & (TOK - 1)) + row_index * TOK
    key_prompt = jnp.zeros((1, keys), jnp.int32)
    for h in range(GROUPS):
        item = prefix_item[h * GROUPS + group]
        here = (lane >> 4) == h
        key_pos = key_pos + jnp.where(here, (item & (MAXPAGES - 1)) * PAGE, 0)
        key_prompt = jnp.where(here, (item >> 3) - group * 2, key_prompt)
    usable = (key_prompt == row_prompt) & (key_pos < prompt_lens)
    offset = (key_pos - query_pos).astype(f32)
    col = iota((ROWS, ROWS), 1)
    new_usable = ((col >> 1) == (row >> 1)) & ((col & 1) <= (row & 1)) & (row_index == 0)
    new_offset = ((col & 1) - (row & 1)).astype(f32)
    stats = jnp.zeros((ROWS, 128), f32)
    for head in range(HEADS):
        at = slice(head * HD, (head + 1) * HD)
        q = fresh[:, head * HD : (head + 1) * HD]
        new_k = fresh[:, WIDE + head * HD : WIDE + (head + 1) * HD]
        new_v = fresh[:, 2 * WIDE + head * HD : 2 * WIDE + (head + 1) * HD]
        k = recv[:, 0:TOK, at].reshape(keys, HD)
        v = recv[:, TOK : 2 * TOK, at].reshape(keys, HD)
        slope = slope_of(first_head + head)
        scores = dot_t(q, k) * (1.0 / math.sqrt(HD)) + slope * offset
        scores = jnp.where(usable, scores, masked_score)
        new_scores = dot_t(q, new_k) * (1.0 / math.sqrt(HD)) + slope * new_offset
        new_scores = jnp.where(new_usable, new_scores, masked_score)
        m = rounded(
            jnp.maximum(
                jnp.max(scores, axis=1, keepdims=True),
                jnp.max(new_scores, axis=1, keepdims=True),
            )
        )
        weights = jnp.where(usable, jnp.exp(scores - m), 0.0)
        new_weights = jnp.where(new_usable, jnp.exp(new_scores - m), 0.0)
        total = jnp.sum(weights, axis=1, keepdims=True) + jnp.sum(
            new_weights, axis=1, keepdims=True
        )
        stats = put_stats(stats, head, m, total)
        out[:, at] = dot(weights.astype(bf16), v) + dot(new_weights.astype(bf16), new_v)
    out[:, WIDE:PACK] = stats


def join_kernel(tail_item, prefix, recv, out, wide):
    group = lax.axis_index("pages")
    for h in range(GROUPS):
        wide[4 * h : 4 * h + 4] = recv[h].astype(f32)
    lane = iota((1, ROWS), 1)
    target = lane & 1
    for j in range(TAILS):
        item = tail_item[(j // 2) * TAILS + group * 2 + j % 2] - group * TAILS
        target = target + jnp.where((lane >> 1) == j, item * 2, 0)
    order = one_hot(iota((ROWS, ROWS), 0) == target)
    tails = dot(order, wide[...].astype(bf16))
    tail_stats = tails[:, WIDE:PACK]
    prefix_stats = prefix[:, WIDE:PACK]
    stats = jnp.zeros((ROWS, 128), f32)
    for head in range(HEADS):
        at = slice(head * HD, (head + 1) * HD)
        left_m, left_l = get_stats(prefix_stats, head)
        right_m, right_l = get_stats(tail_stats, head)
        m = jnp.maximum(left_m, right_m)
        left = jnp.exp(left_m - m)
        right = jnp.exp(right_m - m)
        stats = put_stats(stats, head, m, left * left_l + right * right_l)
        joined = (left * prefix[:, at] + right * tails[:, at]).astype(bf16)
        for n in range(NROW):
            out[n, :, at] = joined
    stats = stats.astype(bf16)
    for n in range(NROW):
        out[n, :, WIDE:PACK] = stats


def out_kernel(recv, weight, base, out, wide):
    stats = [recv[n, :, WIDE:PACK].astype(f32) for n in range(NROW)]
    for head in range(HEADS):
        at = slice(head * HD, (head + 1) * HD)
        parts = [get_stats(s, head) for s in stats]
        m = parts[0][0]
        for part in parts[1:]:
            m = jnp.maximum(m, part[0])
        total = jnp.zeros((ROWS, 1), f32)
        attended = jnp.zeros((ROWS, HD), f32)
        for n in range(NROW):
            scale = jnp.exp(parts[n][0] - m)
            total = total + scale * parts[n][1]
            attended = attended + scale * recv[n, :, at].astype(f32)
        wide[:, at] = (attended / total).astype(bf16)
    partial = (dot(wide[...], weight[...]) + base[...]).astype(bf16)
    for n in range(NCOL):
        out[n] = partial


def centred(values, gain):
    mean = jnp.mean(values, axis=1, keepdims=True)
    away = values - mean
    return mean, jnp.sum(away * away, axis=1, keepdims=True), (away * gain).astype(bf16)


def as_rows(columns):
    lane = iota((ROWS, 8), 1)
    table = jnp.zeros((ROWS, 8), f32)
    for at, column in columns:
        table = jnp.where(lane == at, column, table)
    eye = one_hot(iota((ROWS, ROWS), 0) == iota((ROWS, ROWS), 1))
    return lax.dot_general(
        table.astype(bf16), eye, (((0,), (0,)), ((), ())), preferred_element_type=f32
    )


def up_kernel(recv, vectors, extra, weight, hidden, out):
    values = recv[0].astype(f32)
    for n in range(1, NCOL):
        values = values + recv[n].astype(f32)
    hidden[...] = values
    mean, spread, scaled = centred(values, vectors[0:1])
    rows = as_rows(list(zip((4, 5, 6, 7), split(mean) + split(spread))))
    rows = jnp.concatenate([rows, jnp.zeros((8, BLOCK - ROWS), f32)], axis=1)
    edge = iota((8, BLOCK), 0)
    for n in range(NROW):
        out[n, 0:ROWS] = dot(scaled, weight[:, n * BLOCK : (n + 1) * BLOCK]).astype(bf16)
        out[n, ROWS : ROWS + 8] = jnp.where(edge < 4, extra[n], rows).astype(bf16)


def as_columns(recv):
    rows = jnp.concatenate([recv[n, ROWS : ROWS + 8, 0:ROWS].astype(f32) for n in range(NROW)], 0)
    eye = one_hot(iota((ROWS, ROWS), 0) == iota((ROWS, ROWS), 1))
    return dot_t(eye, rows.astype(bf16))


def scale_of(means, spreads):
    mean = sum(means) / NROW
    spread = sum(spreads)
    for part in means:
        spread = spread + BLOCK * (part - mean) * (part - mean)
    return mean, lax.rsqrt(spread / D + norm_eps)


def projected(recv, width, bias, gain_at, shift_at, mean_at, spread_at):
    columns = as_columns(recv)

    def column(n, at):
        return columns[:, 8 * n + at : 8 * n + at + 1] + columns[:, 8 * n + at + 1 : 8 * n + at + 2]

    means = [column(n, mean_at) for n in range(NROW)]
    mean, scale = scale_of(means, [column(n, spread_at) for n in range(NROW)])
    total = jnp.zeros((ROWS, width), f32)
    shifted = bias
    for n in range(NROW):
        edge = recv[n, ROWS : ROWS + 8].astype(f32)
        gained = sum(edge[at : at + 1] for at in gain_at)
        shifted = shifted + sum(edge[at : at + 1] for at in shift_at)
        total = total + recv[n, 0:ROWS].astype(f32) + (means[n] - mean) * gained
    return total * scale + shifted


def hidden_kernel(recv, vectors, out):
    v = projected(recv, BLOCK, vectors[4:5], (0, 1), (2, 3), 4, 6)
    v = 0.5 * v * (1.0 + jnp.tanh(math.sqrt(2.0 / math.pi) * (v + 0.044715 * (v * v * v))))
    v = v.astype(bf16)
    for n in range(NROW):
        out[n] = v


def down_kernel(recv, weight, vectors, out):
    total = vectors[3:4]
    for n in range(NROW):
        total = total + dot(recv[n], weight[n * BLOCK : (n + 1) * BLOCK])
    total = total.astype(bf16)
    for n in range(NCOL):
        out[n] = total


def next_kernel(recv, hidden, vectors, extra, weight, layer_out, out):
    values = hidden[...]
    for n in range(NCOL):
        values = values + recv[n].astype(f32)
    low = values.astype(bf16)
    values = low.astype(f32)
    layer_out[...] = dot_t(low, own_columns()).astype(bf16)
    mean, spread, scaled = centred(values, vectors[1:2])
    scores = jnp.sum(values * vectors[2:3], axis=1, keepdims=True)
    rows = as_rows(list(zip((2, 3, 4, 5, 6, 7), split(mean) + split(spread) + split(scores))))
    width = out.shape[2]
    rows = jnp.concatenate([rows, jnp.zeros((8, width - ROWS), f32)], axis=1)
    edge = iota((8, width), 0)
    for n in range(NROW):
        out[n, 0:ROWS] = dot(scaled, weight[:, n * width : (n + 1) * width]).astype(bf16)
        out[n, ROWS : ROWS + 8] = jnp.where(edge < 2, extra[n], rows).astype(bf16)


def final_kernel(recv, vectors, projected_next, score_out, wide):
    width = projected_next.shape[2]
    wide[...] = projected(recv, width, vectors[5:6, 0:width], (0,), (1,), 2, 4)
    for i in range(ROWS // 2):
        projected_next[i] = wide[2 * i : 2 * i + 2].astype(bf16)
    total = jnp.zeros((1, ROWS), f32)
    for n in range(NROW):
        edge = recv[n, ROWS : ROWS + 8, 0:ROWS].astype(f32)
        total = total + edge[6:7] + edge[7:8]
    hi, rest = split(total)
    mid, low = split(rest)
    row = iota((8, ROWS), 0)
    parts = jnp.where(row == 0, hi, jnp.where(row == 1, mid, jnp.where(row == 2, low, 0.0)))
    source = iota((ROWS, ROWS // 2), 0)
    target = iota((ROWS, ROWS // 2), 1) * 2
    for u in range(2):
        taken = dot(parts.astype(bf16), one_hot(source == target + u))
        score_out[u : u + 1] = taken[0:1] + taken[1:2] + taken[2:3]


def call(kernel, out, scalars, arrays, scratch=(), remote=()):
    many = isinstance(out, list)
    outs = out if many else [out]
    moved = sum(a.size * a.dtype.itemsize for a in arrays)
    moved += sum(math.prod(s) * jnp.dtype(t).itemsize for s, t in outs)
    shapes = [jax.ShapeDtypeStruct(s, t) for s, t in outs]
    vmem = pl.BlockSpec(memory_space=pltpu.VMEM)
    specs = [pl.BlockSpec(memory_space=pltpu.HBM)] * len(remote)
    specs += [pl.BlockSpec(memory_space=pltpu.SMEM)] * len(scalars) + [vmem] * len(arrays)
    return pl.pallas_call(
        kernel,
        out_shape=shapes if many else shapes[0],
        in_specs=specs,
        out_specs=[vmem] * len(outs) if many else vmem,
        scratch_shapes=scratch,
        cost_estimate=pl.CostEstimate(flops=0, bytes_accessed=moved, transcendentals=0),
        compiler_params=pltpu.CompilerParams(vmem_limit_bytes=24 * 1024 * 1024),
        name=kernel.__name__,
    )(*remote, *scalars, *arrays)


def exchange(x, axis):
    return lax.all_to_all(x, axis, split_axis=0, concat_axis=0, tiled=True)


def shards(
    residual,
    fresh_qkv,
    prefix_pages,
    tail_pages,
    prefix_item,
    tail_item,
    prefix_length,
    tail_length,
    out_weight,
    out_bias,
    mlp_gain,
    mlp_shift,
    up_weight,
    up_bias,
    down_weight,
    down_bias,
    next_gain,
    next_shift,
    score_weight,
    qkv_weight,
    qkv_bias,
):
    cont_local = residual.shape[0]
    share = residual.shape[2]
    width = qkv_bias.shape[0]

    small = jnp.concatenate(
        [
            mlp_gain,
            mlp_shift,
            next_gain,
            next_shift,
            score_weight,
            up_bias,
            qkv_bias,
            out_bias,
            down_bias,
            jnp.zeros((192,), bf16),
        ]
    ).reshape(16, 128)
    stored = jnp.swapaxes(fresh_qkv, 1, 2).reshape(cont_local, 3, 2, WIDE)
    sent = call(
        send_kernel,
        ((GROUPS, 2 * TOK + 4, WIDE), bf16),
        [],
        [],
        [
            pltpu.SMEM(tail_item.shape, jnp.int32),
            pltpu.VMEM((cont_local, 2, WIDE), bf16),
            pltpu.VMEM((ROWS, WIDE), f32),
            pltpu.SemaphoreType.DMA((3,)),
        ],
        [tail_item, stored, prefix_pages.reshape(GROUPS, 2 * TOK, WIDE)],
    )
    arrived = exchange(sent, "pages")
    tails = call(
        tail_kernel,
        ((GROUPS, 4, PACK), bf16),
        [tail_item, tail_length],
        [arrived, tail_pages],
        [pltpu.VMEM((ROWS, PACK), f32)],
    )
    tails = exchange(tails, "pages")
    prefix, base, vectors, up_rows, qkv_rows = call(
        prefix_kernel,
        [
            ((ROWS, PACK), f32),
            ((ROWS, BLOCK), f32),
            ((8, BLOCK), f32),
            ((NROW, 8, BLOCK), f32),
            ((NROW, 8, width), f32),
        ],
        [prefix_item, prefix_length, tail_length],
        [
            fresh_qkv.reshape(ROWS, 3 * WIDE),
            arrived,
            residual.reshape(ROWS, share),
            small,
            up_weight,
            qkv_weight,
        ],
    )
    joined = call(
        join_kernel,
        ((NROW, ROWS, PACK), bf16),
        [tail_item],
        [prefix, tails],
        [pltpu.VMEM((ROWS, PACK), f32)],
    )
    joined = exchange(joined, "row")
    partial = call(
        out_kernel,
        ((NCOL, ROWS, BLOCK), bf16),
        [],
        [joined, out_weight, base],
        [pltpu.VMEM((ROWS, WIDE), bf16)],
    )
    partial = exchange(partial, "col")
    hidden_one, partial = call(
        up_kernel,
        [((ROWS, BLOCK), f32), ((NROW, ROWS + 8, BLOCK), bf16)],
        [],
        [partial, vectors, up_rows, up_weight],
    )
    partial = exchange(partial, "row")
    hidden_two = call(hidden_kernel, ((NROW, ROWS, BLOCK), bf16), [], [partial, vectors])
    hidden_two = exchange(hidden_two, "row")
    partial = call(
        down_kernel, ((NCOL, ROWS, BLOCK), bf16), [], [hidden_two, down_weight, vectors]
    )
    partial = exchange(partial, "col")
    layer_out, partial = call(
        next_kernel,
        [((ROWS, share), bf16), ((NROW, ROWS + 8, width), bf16)],
        [],
        [partial, hidden_one, vectors, qkv_rows, qkv_weight],
    )
    partial = exchange(partial, "row")
    projected_next, score_sum = call(
        final_kernel,
        [((cont_local, 2, width), bf16), ((2, cont_local), f32)],
        [],
        [partial, vectors],
        [pltpu.VMEM((ROWS, width), f32)],
    )
    return (layer_out.reshape(cont_local, 2, share), score_sum.T, projected_next)


def solution(mesh):
    in_specs = (
        P("pages", None, ("row", "col")),
        P("pages", None, None, "col"),
        P("pages", None, "row", "col"),
        P("pages", None, "row", "col"),
        P(),
        P(),
        P(),
        P(),
        P("col", "row"),
        P(("row", "col")),
        P("row"),
        P("row"),
        P("row", "col"),
        P(("col", "row")),
        P("col", "row"),
        P(("row", "col")),
        P("row"),
        P("row"),
        P("row"),
        P("row", "col"),
        P(("col", "row")),
    )
    out_specs = (
        P("pages", None, ("row", "col")),
        P("pages", None),
        P("pages", None, ("col", "row")),
    )
    return jax.shard_map(shards, mesh=mesh, in_specs=in_specs, out_specs=out_specs, check_vma=False)
```

```python
import math

import jax
import jax.numpy as jnp
from jax import lax
from jax.experimental import pallas as pl
from jax.experimental.pallas import tpu as pltpu
from jax.sharding import PartitionSpec as P

D = 2048
H = 16
HD = 128
PAGE = 128
MAXPAGES = 8
CONT = 16

GROUPS = 16
NROW = 8
NCOL = 4
ROWS = 64
HEADS = 4
WIDE = HEADS * HD
PACK = WIDE + 128
BLOCK = D // NROW
TOK = 16
TAILS = 32
KEYROWS = 2 * HEADS * TOK

masked_score = -1e30
norm_eps = 1e-05
f32 = jnp.float32
bf16 = jnp.bfloat16


def dot(a, b):
    return jnp.dot(a, b, preferred_element_type=f32)


def dot_t(a, b):
    return lax.dot_general(a, b, (((1,), (1,)), ((), ())), preferred_element_type=f32)


def iota(shape, dim):
    return lax.broadcasted_iota(jnp.int32, shape, dim)


def one_hot(mask):
    return jnp.where(mask, 1.0, 0.0).astype(bf16)


def rounded(x):
    return x.astype(bf16).astype(f32)


def slope_of(head):
    return jnp.exp2(jnp.full((ROWS, 1), -8.0 / H, f32) * (head + 1).astype(f32))


def put_stats(stats, head, m, l):
    lane = iota((ROWS, 128), 1)
    hi = rounded(l)
    stats = jnp.where(lane == head * 4, m, stats)
    stats = jnp.where(lane == head * 4 + 1, hi, stats)
    return jnp.where(lane == head * 4 + 2, l - hi, stats)


def get_stats(stats, head):
    at = head * 4
    return stats[:, at : at + 1], stats[:, at + 1 : at + 2] + stats[:, at + 2 : at + 3]


def send_kernel(tail_item, fresh, pages, out, items, query, wide, rows, stage, sems, out_sems):
    copies = [
        pltpu.make_async_copy(tail_item, items, sems.at[0]),
        pltpu.make_async_copy(fresh.at[:, 0], query, sems.at[1]),
    ]
    for n in range(2 * HEADS):
        head = slice((n % HEADS) * HD, (n % HEADS + 1) * HD)
        copies.append(
            pltpu.make_async_copy(
                pages.at[:, n // HEADS, :, head],
                stage.at[:, n * TOK : (n + 1) * TOK],
                sems.at[2 + n],
            )
        )
    for copy in copies:
        copy.start()
    group = lax.axis_index("pages")
    source, lane = iota((128, ROWS), 0), iota((128, ROWS), 1)
    place = (((lane >> 2) & 3) == (source >> 5)) & (
        (source & (TAILS - 1)) == group * 2 + ((lane >> 1) & 1)
    )
    place = one_hot(place)
    copies[0].wait()
    local = (items[...] & (TAILS - 1)).astype(f32).astype(bf16)
    found = dot(local, place)
    here = iota(found.shape, 0) == (iota(found.shape, 1) >> 4)
    target = jnp.sum(jnp.where(here, found, 0.0), axis=0, keepdims=True).astype(jnp.int32) * 2
    target = target + (iota((1, ROWS), 1) & 1)
    pick = one_hot(iota((ROWS, ROWS), 0) == target)
    copies[1].wait()
    for j in range(TAILS):
        wide[2 * j : 2 * j + 2] = query[j].astype(f32)
    leaving = []
    for n in range(2 * HEADS):
        part = slice(n * TOK, (n + 1) * TOK)
        copies[2 + n].wait()
        leaving.append(pltpu.make_async_copy(stage.at[:, part], out.at[:, part], out_sems.at[n]))
        leaving[n].start()
    picked = lax.dot_general(
        pick, wide[...].astype(bf16), (((0,), (0,)), ((), ())), preferred_element_type=f32
    )
    for h in range(GROUPS):
        for head in range(HEADS):
            at = h * TOK + head * 4
            rows[at : at + 4] = picked[4 * h : 4 * h + 4, head * HD : (head + 1) * HD]
    stage[:, KEYROWS:] = rows[...].reshape(GROUPS, TOK, HD).astype(bf16)
    last = pltpu.make_async_copy(
        stage.at[:, KEYROWS : KEYROWS + TOK],
        out.at[:, KEYROWS : KEYROWS + TOK],
        out_sems.at[2 * HEADS],
    )
    last.start()
    for copy in leaving + [last]:
        copy.wait()


def own_columns():
    share = BLOCK // NCOL
    first = lax.axis_index("col") * share
    return one_hot(iota((share, BLOCK), 1) == iota((share, BLOCK), 0) + first)


def gain_rows(gain, shift):
    row = iota((16, BLOCK), 0)
    return jnp.where(row == 0, gain, jnp.where(row == 1, shift, 0.0)).astype(bf16)


def split(x):
    hi = rounded(x)
    return hi, x - hi


def ready_kernel(
    tail_item,
    tail_length,
    prefix_item,
    prefix_length,
    residual,
    small,
    tail_offset,
    prefix_offset,
    order,
    base,
    vectors,
):
    group = lax.axis_index("pages")
    row_index = lax.axis_index("row")
    row = iota((ROWS, 1), 0)
    step = row & 1
    lens = jnp.zeros((ROWS, 1), jnp.int32)
    own_lens = jnp.zeros((ROWS, 1), jnp.int32)
    lane = iota((1, ROWS), 1)
    target = lane & 1
    for j in range(TAILS):
        here = (row >> 1) == j
        lens = jnp.where(here, tail_length[tail_item[group * TAILS + j]], lens)
        own_lens = jnp.where(here, tail_length[group * TAILS + j], own_lens)
        item = tail_item[(j // 2) * TAILS + group * 2 + j % 2] - group * TAILS
        target = target + jnp.where((lane >> 1) == j, item * 2, 0)
    order[...] = one_hot(iota((ROWS, ROWS), 0) == target)

    key = iota((ROWS, 8 * TOK), 1)
    token = (key & (TOK - 1)) + row_index * TOK
    usable = ((key >> 4) == ((row >> 1) & 7)) & (token < lens)
    offset = (token - lens - step).astype(f32)
    tail_offset[...] = jnp.where(usable, offset, masked_score)

    row_prompt = row >> 5
    prompt_lens = jnp.where(
        row_prompt == 0, prefix_length[group * 2], prefix_length[group * 2 + 1]
    )
    query_pos = prompt_lens + own_lens + step
    lane = iota((1, GROUPS * TOK), 1)
    key_pos = (lane & (TOK - 1)) + row_index * TOK
    key_prompt = jnp.zeros((1, GROUPS * TOK), jnp.int32)
    for h in range(GROUPS):
        item = prefix_item[h * GROUPS + group]
        here = (lane >> 4) == h
        key_pos = key_pos + jnp.where(here, (item & (MAXPAGES - 1)) * PAGE, 0)
        key_prompt = jnp.where(here, (item >> 3) - group * 2, key_prompt)
    usable = (key_prompt == row_prompt) & (key_pos < prompt_lens)
    offset = (key_pos - query_pos).astype(f32)
    prefix_offset[...] = jnp.where(usable, offset, masked_score)

    table = small[...].astype(f32)

    def line(at):
        return jnp.concatenate([table[at : at + 1], table[at + 1 : at + 2]], axis=1)

    share = BLOCK // NCOL
    place = own_columns()

    def placed(values):
        return dot(jnp.broadcast_to(values, (8, share)).astype(bf16), place)[0:1]

    base[...] = dot(residual[...], place) + placed(table[13:14, 64:128])
    rows = [line(0), line(4), line(8), placed(table[14:15, 0:64]), line(10), line(12), line(2), line(6)]
    edge = iota((8, BLOCK), 0)
    filled = jnp.zeros((8, BLOCK), f32)
    for at, values in enumerate(rows):
        filled = jnp.where(edge == at, values, filled)
    vectors[...] = filled


def tail_kernel(recv, tails, distance, out, query, wide):
    first_head = lax.axis_index("col") * HEADS
    distance = distance[...]
    usable = distance > 0.5 * masked_score
    for g in range(GROUPS):
        rows = recv[g, KEYROWS:].astype(f32)
        for head in range(HEADS):
            query[head, 4 * g : 4 * g + 4] = rows[4 * head : 4 * head + 4]
    some = ROWS * 8 // TAILS
    blocks = ROWS // some
    stats = jnp.zeros((ROWS, 128), f32)
    for head in range(HEADS):
        at = slice(head * HD, (head + 1) * HD)
        q = query[head].astype(bf16)
        parts = []
        for n in range(blocks):
            k = tails[8 * n : 8 * n + 8, 0, :, at].reshape(8 * TOK, HD)
            parts.append(dot_t(q[n * some : (n + 1) * some], k))
        scores = jnp.concatenate(parts, axis=0) * (1.0 / math.sqrt(HD))
        scores = scores + slope_of(first_head + head) * distance
        scores = jnp.where(usable, scores, masked_score)
        m = rounded(jnp.max(scores, axis=1, keepdims=True))
        weights = jnp.where(usable, jnp.exp(scores - m), 0.0)
        stats = put_stats(stats, head, m, jnp.sum(weights, axis=1, keepdims=True))
        weights = weights.astype(bf16)
        for n in range(blocks):
            v = tails[8 * n : 8 * n + 8, 1, :, at].reshape(8 * TOK, HD)
            wide[n * some : (n + 1) * some, at] = dot(weights[n * some : (n + 1) * some], v)
    wide[:, WIDE:PACK] = stats
    for g in range(GROUPS):
        out[g] = wide[4 * g : 4 * g + 4].astype(bf16)


def prefix_kernel(
    fresh, recv, distance, vectors, up_weight, qkv_weight, out, up_rows, qkv_rows
):
    both = gain_rows(vectors[0:1], vectors[6:7])
    edge = iota((8, BLOCK), 0)
    for n in range(NROW):
        parts = dot(both, up_weight[:, n * BLOCK : (n + 1) * BLOCK])
        rows = jnp.zeros((8, BLOCK), f32)
        for at, values in enumerate(split(parts[0:1]) + split(parts[1:2])):
            rows = jnp.where(edge == at, values, rows)
        up_rows[n] = rows
    both = gain_rows(vectors[1:2], vectors[7:8])
    width = qkv_rows.shape[2]
    for n in range(NROW):
        qkv_rows[n] = dot(both, qkv_weight[:, n * width : (n + 1) * width])[0:8]

    distance = distance[...]
    usable = distance > 0.5 * masked_score
    row_index = lax.axis_index("row")
    first_head = lax.axis_index("col") * HEADS
    row = iota((ROWS, 1), 0)
    keys = GROUPS * TOK
    col = iota((ROWS, ROWS), 1)
    new_usable = ((col >> 1) == (row >> 1)) & ((col & 1) <= (row & 1)) & (row_index == 0)
    new_offset = ((col & 1) - (row & 1)).astype(f32)
    stats = jnp.zeros((ROWS, 128), f32)
    for head in range(HEADS):
        at = slice(head * HD, (head + 1) * HD)
        q = fresh[:, head * HD : (head + 1) * HD]
        new_k = fresh[:, WIDE + head * HD : WIDE + (head + 1) * HD]
        new_v = fresh[:, 2 * WIDE + head * HD : 2 * WIDE + (head + 1) * HD]
        k = recv[:, head * TOK : (head + 1) * TOK].reshape(keys, HD)
        v = recv[:, (HEADS + head) * TOK : (HEADS + head + 1) * TOK].reshape(keys, HD)
        slope = slope_of(first_head + head)
        scores = dot_t(q, k) * (1.0 / math.sqrt(HD)) + slope * distance
        scores = jnp.where(usable, scores, masked_score)
        new_scores = dot_t(q, new_k) * (1.0 / math.sqrt(HD)) + slope * new_offset
        new_scores = jnp.where(new_usable, new_scores, masked_score)
        m = rounded(
            jnp.maximum(
                jnp.max(scores, axis=1, keepdims=True),
                jnp.max(new_scores, axis=1, keepdims=True),
            )
        )
        weights = jnp.where(usable, jnp.exp(scores - m), 0.0)
        new_weights = jnp.where(new_usable, jnp.exp(new_scores - m), 0.0)
        total = jnp.sum(weights, axis=1, keepdims=True) + jnp.sum(
            new_weights, axis=1, keepdims=True
        )
        stats = put_stats(stats, head, m, total)
        out[:, at] = dot(weights.astype(bf16), v) + dot(new_weights.astype(bf16), new_v)
    out[:, WIDE:PACK] = stats


def join_kernel(order, prefix, recv, out, wide):
    for h in range(GROUPS):
        wide[4 * h : 4 * h + 4] = recv[h].astype(f32)
    tails = dot(order[...], wide[...].astype(bf16))
    tail_stats = tails[:, WIDE:PACK]
    prefix_stats = prefix[:, WIDE:PACK]
    stats = jnp.zeros((ROWS, 128), f32)
    for head in range(HEADS):
        at = slice(head * HD, (head + 1) * HD)
        left_m, left_l = get_stats(prefix_stats, head)
        right_m, right_l = get_stats(tail_stats, head)
        m = jnp.maximum(left_m, right_m)
        left = jnp.exp(left_m - m)
        right = jnp.exp(right_m - m)
        stats = put_stats(stats, head, m, left * left_l + right * right_l)
        joined = (left * prefix[:, at] + right * tails[:, at]).astype(bf16)
        for n in range(NROW):
            out[n, :, at] = joined
    stats = stats.astype(bf16)
    for n in range(NROW):
        out[n, :, WIDE:PACK] = stats


def out_kernel(recv, weight, base, out, wide):
    stats = [recv[n, :, WIDE:PACK].astype(f32) for n in range(NROW)]
    for head in range(HEADS):
        at = slice(head * HD, (head + 1) * HD)
        parts = [get_stats(s, head) for s in stats]
        m = parts[0][0]
        for part in parts[1:]:
            m = jnp.maximum(m, part[0])
        total = jnp.zeros((ROWS, 1), f32)
        attended = jnp.zeros((ROWS, HD), f32)
        for n in range(NROW):
            scale = jnp.exp(parts[n][0] - m)
            total = total + scale * parts[n][1]
            attended = attended + scale * recv[n, :, at].astype(f32)
        wide[:, at] = (attended / total).astype(bf16)
    partial = (dot(wide[...], weight[...]) + base[...]).astype(bf16)
    for n in range(NCOL):
        out[n] = partial


def centred(values, gain):
    mean = jnp.mean(values, axis=1, keepdims=True)
    away = values - mean
    return mean, jnp.sum(away * away, axis=1, keepdims=True), (away * gain).astype(bf16)


def as_rows(columns, order=None):
    lane = iota((ROWS, 8), 1)
    table = jnp.zeros((ROWS, 8), f32)
    for at, column in columns:
        table = jnp.where(lane == at, column, table)
    if order is None:
        order = iota((ROWS, ROWS), 1)
    order = one_hot(iota((ROWS, ROWS), 0) == order)
    return lax.dot_general(
        table.astype(bf16), order, (((0,), (0,)), ((), ())), preferred_element_type=f32
    )


def up_kernel(recv, vectors, extra, weight, hidden, out):
    values = recv[0].astype(f32)
    for n in range(1, NCOL):
        values = values + recv[n].astype(f32)
    hidden[...] = values
    mean, spread, scaled = centred(values, vectors[0:1])
    rows = as_rows(list(zip((4, 5, 6, 7), split(mean) + split(spread))))
    rows = jnp.concatenate([rows, jnp.zeros((8, BLOCK - ROWS), f32)], axis=1)
    edge = iota((8, BLOCK), 0)
    for n in range(NROW):
        out[n, 0:ROWS] = dot(scaled, weight[:, n * BLOCK : (n + 1) * BLOCK]).astype(bf16)
        out[n, ROWS : ROWS + 8] = jnp.where(edge < 4, extra[n], rows).astype(bf16)


def as_columns(recv):
    rows = jnp.concatenate([recv[n, ROWS : ROWS + 8, 0:ROWS].astype(f32) for n in range(NROW)], 0)
    eye = one_hot(iota((ROWS, ROWS), 0) == iota((ROWS, ROWS), 1))
    return dot_t(eye, rows.astype(bf16))


def scale_of(means, spreads):
    mean = sum(means) / NROW
    spread = sum(spreads)
    for part in means:
        spread = spread + BLOCK * (part - mean) * (part - mean)
    return mean, lax.rsqrt(spread / D + norm_eps)


def projected(recv, width, bias, gain_at, shift_at, mean_at, spread_at):
    columns = as_columns(recv)

    def column(n, at):
        return columns[:, 8 * n + at : 8 * n + at + 1] + columns[:, 8 * n + at + 1 : 8 * n + at + 2]

    means = [column(n, mean_at) for n in range(NROW)]
    mean, scale = scale_of(means, [column(n, spread_at) for n in range(NROW)])
    total = jnp.zeros((ROWS, width), f32)
    shifted = bias
    for n in range(NROW):
        edge = recv[n, ROWS : ROWS + 8].astype(f32)
        gained = sum(edge[at : at + 1] for at in gain_at)
        shifted = shifted + sum(edge[at : at + 1] for at in shift_at)
        total = total + recv[n, 0:ROWS].astype(f32) + (means[n] - mean) * gained
    return total * scale + shifted


def hidden_kernel(recv, vectors, out):
    v = projected(recv, BLOCK, vectors[4:5], (0, 1), (2, 3), 4, 6)
    v = 0.5 * v * (1.0 + jnp.tanh(math.sqrt(2.0 / math.pi) * (v + 0.044715 * (v * v * v))))
    v = v.astype(bf16)
    for n in range(NROW):
        out[n] = v


def down_kernel(recv, weight, vectors, out):
    total = vectors[3:4]
    for n in range(NROW):
        total = total + dot(recv[n], weight[n * BLOCK : (n + 1) * BLOCK])
    total = total.astype(bf16)
    for n in range(NCOL):
        out[n] = total


def next_kernel(recv, hidden, vectors, extra, weight, layer_out, out):
    values = hidden[...]
    for n in range(NCOL):
        values = values + recv[n].astype(f32)
    low = values.astype(bf16)
    values = low.astype(f32)
    layer_out[...] = dot_t(low, own_columns()).astype(bf16)
    mean, spread, scaled = centred(values, vectors[1:2])
    scores = jnp.sum(values * vectors[2:3], axis=1, keepdims=True)
    lane = iota((ROWS, ROWS), 1)
    by_step = ((lane & 31) << 1) + (lane >> 5)
    rows = as_rows(list(zip((2, 3, 4, 5), split(mean) + split(spread))))
    rows = rows + as_rows(list(zip((6, 7), split(scores))), by_step)
    width = out.shape[2]
    rows = jnp.concatenate([rows, jnp.zeros((8, width - ROWS), f32)], axis=1)
    edge = iota((8, width), 0)
    for n in range(NROW):
        out[n, 0:ROWS] = dot(scaled, weight[:, n * width : (n + 1) * width]).astype(bf16)
        out[n, ROWS : ROWS + 8] = jnp.where(edge < 2, extra[n], rows).astype(bf16)


def final_kernel(recv, vectors, projected_next, score_out, wide):
    width = projected_next.shape[2]
    wide[...] = projected(recv, width, vectors[5:6, 0:width], (0,), (1,), 2, 4)
    for i in range(ROWS // 2):
        projected_next[i] = wide[2 * i : 2 * i + 2].astype(bf16)
    total = jnp.zeros((1, ROWS), f32)
    for n in range(NROW):
        edge = recv[n, ROWS : ROWS + 8, 0:ROWS].astype(f32)
        total = total + edge[6:7] + edge[7:8]
    half = ROWS // 2
    score_out[0:1] = total[:, 0:half]
    score_out[1:2] = total[:, half:]


def call(kernel, out, scalars, arrays, scratch=(), remote=(), limit=16, home=pltpu.VMEM):
    many = isinstance(out, list)
    outs = out if many else [out]
    moved = sum(a.size * a.dtype.itemsize for a in arrays)
    moved += sum(math.prod(s) * jnp.dtype(t).itemsize for s, t in outs)
    shapes = [jax.ShapeDtypeStruct(s, t) for s, t in outs]
    vmem = pl.BlockSpec(memory_space=pltpu.VMEM)
    specs = [pl.BlockSpec(memory_space=pltpu.HBM)] * len(remote)
    specs += [pl.BlockSpec(memory_space=pltpu.SMEM)] * len(scalars) + [vmem] * len(arrays)
    return pl.pallas_call(
        kernel,
        out_shape=shapes if many else shapes[0],
        in_specs=specs,
        out_specs=[vmem] * len(outs) if many else pl.BlockSpec(memory_space=home),
        scratch_shapes=scratch,
        cost_estimate=pl.CostEstimate(flops=0, bytes_accessed=moved, transcendentals=0),
        compiler_params=pltpu.CompilerParams(vmem_limit_bytes=limit * 1024 * 1024),
        name=kernel.__name__,
    )(*remote, *scalars, *arrays)


def exchange(x, axis):
    return lax.all_to_all(x, axis, split_axis=0, concat_axis=0, tiled=True)


def shards(
    residual,
    fresh_qkv,
    prefix_pages,
    tail_pages,
    prefix_item,
    tail_item,
    prefix_length,
    tail_length,
    out_weight,
    out_bias,
    mlp_gain,
    mlp_shift,
    up_weight,
    up_bias,
    down_weight,
    down_bias,
    next_gain,
    next_shift,
    score_weight,
    qkv_weight,
    qkv_bias,
):
    cont_local = residual.shape[0]
    share = residual.shape[2]
    width = qkv_bias.shape[0]

    small = jnp.concatenate(
        [
            mlp_gain,
            mlp_shift,
            next_gain,
            next_shift,
            score_weight,
            up_bias,
            qkv_bias,
            out_bias,
            down_bias,
            jnp.zeros((192,), bf16),
        ]
    ).reshape(16, 128)
    stored = jnp.swapaxes(fresh_qkv, 1, 2).reshape(cont_local, 3, 2, WIDE)
    sent = call(
        send_kernel,
        ((GROUPS, KEYROWS + TOK, HD), bf16),
        [],
        [],
        [
            pltpu.VMEM((4, 128), jnp.int32),
            pltpu.VMEM((cont_local, 2, WIDE), bf16),
            pltpu.VMEM((ROWS, WIDE), f32),
            pltpu.VMEM((GROUPS * TOK, HD), f32),
            pltpu.VMEM((GROUPS, KEYROWS + TOK, HD), bf16),
            pltpu.SemaphoreType.DMA((2 + 2 * HEADS,)),
            pltpu.SemaphoreType.DMA((1 + 2 * HEADS,)),
        ],
        [tail_item.reshape(4, 128), stored, prefix_pages],
        60,
        pltpu.HBM,
    )
    arrived = exchange(sent, "pages")
    tail_offset, prefix_offset, order, base, vectors = call(
        ready_kernel,
        [
            ((ROWS, 8 * TOK), f32),
            ((ROWS, GROUPS * TOK), f32),
            ((ROWS, ROWS), bf16),
            ((ROWS, BLOCK), f32),
            ((8, BLOCK), f32),
        ],
        [tail_item, tail_length, prefix_item, prefix_length],
        [residual.reshape(ROWS, share), small],
    )
    tails = call(
        tail_kernel,
        ((GROUPS, 4, PACK), bf16),
        [],
        [arrived, tail_pages, tail_offset],
        [pltpu.VMEM((HEADS, ROWS, HD), f32), pltpu.VMEM((ROWS, PACK), f32)],
    )
    tails = exchange(tails, "pages")
    prefix, up_rows, qkv_rows = call(
        prefix_kernel,
        [((ROWS, PACK), f32), ((NROW, 8, BLOCK), f32), ((NROW, 8, width), f32)],
        [],
        [
            fresh_qkv.reshape(ROWS, 3 * WIDE),
            arrived,
            prefix_offset,
            vectors,
            up_weight,
            qkv_weight,
        ],
    )
    joined = call(
        join_kernel,
        ((NROW, ROWS, PACK), bf16),
        [],
        [order, prefix, tails],
        [pltpu.VMEM((ROWS, PACK), f32)],
    )
    joined = exchange(joined, "row")
    partial = call(
        out_kernel,
        ((NCOL, ROWS, BLOCK), bf16),
        [],
        [joined, out_weight, base],
        [pltpu.VMEM((ROWS, WIDE), bf16)],
    )
    partial = exchange(partial, "col")
    hidden_one, partial = call(
        up_kernel,
        [((ROWS, BLOCK), f32), ((NROW, ROWS + 8, BLOCK), bf16)],
        [],
        [partial, vectors, up_rows, up_weight],
    )
    partial = exchange(partial, "row")
    hidden_two = call(hidden_kernel, ((NROW, ROWS, BLOCK), bf16), [], [partial, vectors])
    hidden_two = exchange(hidden_two, "row")
    partial = call(
        down_kernel, ((NCOL, ROWS, BLOCK), bf16), [], [hidden_two, down_weight, vectors]
    )
    partial = exchange(partial, "col")
    layer_out, partial = call(
        next_kernel,
        [((ROWS, share), bf16), ((NROW, ROWS + 8, width), bf16)],
        [],
        [partial, hidden_one, vectors, qkv_rows, qkv_weight],
    )
    partial = exchange(partial, "row")
    projected_next, score_sum = call(
        final_kernel,
        [((cont_local, 2, width), bf16), ((2, cont_local), f32)],
        [],
        [partial, vectors],
        [pltpu.VMEM((ROWS, width), f32)],
    )
    return (layer_out.reshape(cont_local, 2, share), score_sum.T, projected_next)


def solution(mesh):
    in_specs = (
        P("pages", None, ("row", "col")),
        P("pages", None, None, "col"),
        P("pages", None, "row", "col"),
        P("pages", None, "row", "col"),
        P(),
        P(),
        P(),
        P(),
        P("col", "row"),
        P(("row", "col")),
        P("row"),
        P("row"),
        P("row", "col"),
        P(("col", "row")),
        P("col", "row"),
        P(("row", "col")),
        P("row"),
        P("row"),
        P("row"),
        P("row", "col"),
        P(("col", "row")),
    )
    out_specs = (
        P("pages", None, ("row", "col")),
        P("pages", None),
        P("pages", None, ("col", "row")),
    )
    return jax.shard_map(shards, mesh=mesh, in_specs=in_specs, out_specs=out_specs, check_vma=False)
```

```python
import math

import jax
import jax.numpy as jnp
from jax import lax
from jax.experimental import pallas as pl
from jax.experimental.pallas import tpu as pltpu
from jax.sharding import PartitionSpec as P

D = 2048
H = 16
HD = 128
PAGE = 128
MAXPAGES = 8
CONT = 16

GROUPS = 16
NROW = 8
NCOL = 4
ROWS = 64
HEADS = 4
WIDE = HEADS * HD
PACK = WIDE + 128
BLOCK = D // NROW
TOK = 16
TAILS = 32
KEYROWS = 2 * HEADS * TOK

masked_score = -1e30
norm_eps = 1e-05
f32 = jnp.float32
bf16 = jnp.bfloat16


def dot(a, b):
    return jnp.dot(a, b, preferred_element_type=f32)


def dot_t(a, b):
    return lax.dot_general(a, b, (((1,), (1,)), ((), ())), preferred_element_type=f32)


def iota(shape, dim):
    return lax.broadcasted_iota(jnp.int32, shape, dim)


def one_hot(mask):
    return jnp.where(mask, 1.0, 0.0).astype(bf16)


def rounded(x):
    return x.astype(bf16).astype(f32)


def slope_of(head):
    return jnp.exp2(jnp.full((ROWS, 1), -8.0 / H, f32) * (head + 1).astype(f32))


def put_stats(stats, head, m, l):
    lane = iota((ROWS, 128), 1)
    hi = rounded(l)
    stats = jnp.where(lane == head * 4, m, stats)
    stats = jnp.where(lane == head * 4 + 1, hi, stats)
    return jnp.where(lane == head * 4 + 2, l - hi, stats)


def get_stats(stats, head):
    at = head * 4
    return stats[:, at : at + 1], stats[:, at + 1 : at + 2] + stats[:, at + 2 : at + 3]


def send_kernel(tail_item, fresh, pages, out, items, query, wide, rows, stage, sems, out_sems):
    copies = [
        pltpu.make_async_copy(tail_item, items, sems.at[0]),
        pltpu.make_async_copy(fresh.at[:, 0], query, sems.at[1]),
    ]
    for n in range(2 * HEADS):
        head = slice((n % HEADS) * HD, (n % HEADS + 1) * HD)
        copies.append(
            pltpu.make_async_copy(
                pages.at[:, n // HEADS, :, head],
                stage.at[:, n * TOK : (n + 1) * TOK],
                sems.at[2 + n],
            )
        )
    for copy in copies:
        copy.start()
    group = lax.axis_index("pages")
    source, lane = iota((128, ROWS), 0), iota((128, ROWS), 1)
    place = (((lane >> 2) & 3) == (source >> 5)) & (
        (source & (TAILS - 1)) == group * 2 + ((lane >> 1) & 1)
    )
    place = one_hot(place)
    copies[0].wait()
    local = (items[...] & (TAILS - 1)).astype(f32).astype(bf16)
    found = dot(local, place)
    here = iota(found.shape, 0) == (iota(found.shape, 1) >> 4)
    target = jnp.sum(jnp.where(here, found, 0.0), axis=0, keepdims=True).astype(jnp.int32) * 2
    target = target + (iota((1, ROWS), 1) & 1)
    pick = one_hot(iota((ROWS, ROWS), 0) == target)
    copies[1].wait()
    for j in range(TAILS):
        wide[2 * j : 2 * j + 2] = query[j].astype(f32)
    leaving = []
    for n in range(2 * HEADS):
        part = slice(n * TOK, (n + 1) * TOK)
        copies[2 + n].wait()
        leaving.append(pltpu.make_async_copy(stage.at[:, part], out.at[:, part], out_sems.at[n]))
        leaving[n].start()
    picked = lax.dot_general(
        pick, wide[...].astype(bf16), (((0,), (0,)), ((), ())), preferred_element_type=f32
    )
    for h in range(GROUPS):
        for head in range(HEADS):
            at = h * TOK + head * 4
            rows[at : at + 4] = picked[4 * h : 4 * h + 4, head * HD : (head + 1) * HD]
    stage[:, KEYROWS:] = rows[...].reshape(GROUPS, TOK, HD).astype(bf16)
    last = pltpu.make_async_copy(
        stage.at[:, KEYROWS : KEYROWS + TOK],
        out.at[:, KEYROWS : KEYROWS + TOK],
        out_sems.at[2 * HEADS],
    )
    last.start()
    for copy in leaving + [last]:
        copy.wait()


def own_columns():
    share = BLOCK // NCOL
    first = lax.axis_index("col") * share
    return one_hot(iota((share, BLOCK), 1) == iota((share, BLOCK), 0) + first)


def gain_rows(gain, shift):
    row = iota((16, BLOCK), 0)
    return jnp.where(row == 0, gain, jnp.where(row == 1, shift, 0.0)).astype(bf16)


def split(x):
    hi = rounded(x)
    return hi, x - hi


def ready_kernel(
    tail_item,
    tail_length,
    prefix_item,
    prefix_length,
    residual,
    small,
    tail_offset,
    prefix_offset,
    order,
    base,
    vectors,
):
    group = lax.axis_index("pages")
    row_index = lax.axis_index("row")
    row = iota((ROWS, 1), 0)
    step = row & 1
    lens = jnp.zeros((ROWS, 1), jnp.int32)
    own_lens = jnp.zeros((ROWS, 1), jnp.int32)
    lane = iota((1, ROWS), 1)
    target = lane & 1
    for j in range(TAILS):
        here = (row >> 1) == j
        lens = jnp.where(here, tail_length[tail_item[group * TAILS + j]], lens)
        own_lens = jnp.where(here, tail_length[group * TAILS + j], own_lens)
        item = tail_item[(j // 2) * TAILS + group * 2 + j % 2] - group * TAILS
        target = target + jnp.where((lane >> 1) == j, item * 2, 0)
    order[...] = one_hot(iota((ROWS, ROWS), 0) == target)

    key = iota((ROWS, 8 * TOK), 1)
    token = (key & (TOK - 1)) + row_index * TOK
    usable = ((key >> 4) == ((row >> 1) & 7)) & (token < lens)
    offset = (token - lens - step).astype(f32)
    tail_offset[...] = jnp.where(usable, offset, masked_score)

    row_prompt = row >> 5
    prompt_lens = jnp.where(
        row_prompt == 0, prefix_length[group * 2], prefix_length[group * 2 + 1]
    )
    query_pos = prompt_lens + own_lens + step
    lane = iota((1, GROUPS * TOK), 1)
    key_pos = (lane & (TOK - 1)) + row_index * TOK
    key_prompt = jnp.zeros((1, GROUPS * TOK), jnp.int32)
    for h in range(GROUPS):
        item = prefix_item[h * GROUPS + group]
        here = (lane >> 4) == h
        key_pos = key_pos + jnp.where(here, (item & (MAXPAGES - 1)) * PAGE, 0)
        key_prompt = jnp.where(here, (item >> 3) - group * 2, key_prompt)
    usable = (key_prompt == row_prompt) & (key_pos < prompt_lens)
    offset = (key_pos - query_pos).astype(f32)
    prefix_offset[...] = jnp.where(usable, offset, masked_score)

    table = small[...].astype(f32)

    def line(at):
        return jnp.concatenate([table[at : at + 1], table[at + 1 : at + 2]], axis=1)

    share = BLOCK // NCOL
    place = own_columns()

    def placed(values):
        return dot(jnp.broadcast_to(values, (8, share)).astype(bf16), place)[0:1]

    base[...] = dot(residual[...], place) + placed(table[13:14, 64:128])
    rows = [line(0), line(4), line(8), placed(table[14:15, 0:64]), line(10), line(12), line(2), line(6)]
    edge = iota((8, BLOCK), 0)
    filled = jnp.zeros((8, BLOCK), f32)
    for at, values in enumerate(rows):
        filled = jnp.where(edge == at, values, filled)
    vectors[...] = filled


def tail_kernel(recv, tails, distance, out, query, wide):
    first_head = lax.axis_index("col") * HEADS
    distance = distance[...]
    usable = distance > 0.5 * masked_score
    for g in range(GROUPS):
        rows = recv[g, KEYROWS:].astype(f32)
        for head in range(HEADS):
            query[head, 4 * g : 4 * g + 4] = rows[4 * head : 4 * head + 4]
    some = ROWS * 8 // TAILS
    blocks = ROWS // some
    stats = jnp.zeros((ROWS, 128), f32)
    scores, weights = [], []
    for head in range(HEADS):
        at = slice(head * HD, (head + 1) * HD)
        q = query[head].astype(bf16)
        parts = []
        for n in range(blocks):
            k = tails[8 * n : 8 * n + 8, 0, :, at].reshape(8 * TOK, HD)
            parts.append(dot_t(q[n * some : (n + 1) * some], k))
        scores.append(jnp.concatenate(parts, axis=0))
    for head in range(HEADS):
        biased = scores[head] * (1.0 / math.sqrt(HD)) + slope_of(first_head + head) * distance
        biased = jnp.where(usable, biased, masked_score)
        m = rounded(jnp.max(biased, axis=1, keepdims=True))
        shares = jnp.where(usable, jnp.exp(biased - m), 0.0)
        stats = put_stats(stats, head, m, jnp.sum(shares, axis=1, keepdims=True))
        weights.append(shares.astype(bf16))
    for head in range(HEADS):
        at = slice(head * HD, (head + 1) * HD)
        for n in range(blocks):
            v = tails[8 * n : 8 * n + 8, 1, :, at].reshape(8 * TOK, HD)
            rows = slice(n * some, (n + 1) * some)
            wide[rows, at] = dot(weights[head][rows], v)
    wide[:, WIDE:PACK] = stats
    for g in range(GROUPS):
        out[g] = wide[4 * g : 4 * g + 4].astype(bf16)


def prefix_kernel(
    fresh, recv, distance, vectors, up_weight, qkv_weight, out, up_rows, qkv_rows
):
    both = gain_rows(vectors[0:1], vectors[6:7])
    edge = iota((8, BLOCK), 0)
    for n in range(NROW):
        parts = dot(both, up_weight[:, n * BLOCK : (n + 1) * BLOCK])
        rows = jnp.zeros((8, BLOCK), f32)
        for at, values in enumerate(split(parts[0:1]) + split(parts[1:2])):
            rows = jnp.where(edge == at, values, rows)
        up_rows[n] = rows
    both = gain_rows(vectors[1:2], vectors[7:8])
    width = qkv_rows.shape[2]
    for n in range(NROW):
        qkv_rows[n] = dot(both, qkv_weight[:, n * width : (n + 1) * width])[0:8]

    distance = distance[...]
    usable = distance > 0.5 * masked_score
    row_index = lax.axis_index("row")
    first_head = lax.axis_index("col") * HEADS
    row = iota((ROWS, 1), 0)
    keys = GROUPS * TOK
    col = iota((ROWS, ROWS), 1)
    new_usable = ((col >> 1) == (row >> 1)) & ((col & 1) <= (row & 1)) & (row_index == 0)
    new_offset = ((col & 1) - (row & 1)).astype(f32)
    stats = jnp.zeros((ROWS, 128), f32)
    for head in range(HEADS):
        at = slice(head * HD, (head + 1) * HD)
        q = fresh[:, head * HD : (head + 1) * HD]
        new_k = fresh[:, WIDE + head * HD : WIDE + (head + 1) * HD]
        new_v = fresh[:, 2 * WIDE + head * HD : 2 * WIDE + (head + 1) * HD]
        k = recv[:, head * TOK : (head + 1) * TOK].reshape(keys, HD)
        v = recv[:, (HEADS + head) * TOK : (HEADS + head + 1) * TOK].reshape(keys, HD)
        slope = slope_of(first_head + head)
        scores = dot_t(q, k) * (1.0 / math.sqrt(HD)) + slope * distance
        scores = jnp.where(usable, scores, masked_score)
        new_scores = dot_t(q, new_k) * (1.0 / math.sqrt(HD)) + slope * new_offset
        new_scores = jnp.where(new_usable, new_scores, masked_score)
        m = rounded(
            jnp.maximum(
                jnp.max(scores, axis=1, keepdims=True),
                jnp.max(new_scores, axis=1, keepdims=True),
            )
        )
        weights = jnp.where(usable, jnp.exp(scores - m), 0.0)
        new_weights = jnp.where(new_usable, jnp.exp(new_scores - m), 0.0)
        total = jnp.sum(weights, axis=1, keepdims=True) + jnp.sum(
            new_weights, axis=1, keepdims=True
        )
        stats = put_stats(stats, head, m, total)
        out[:, at] = dot(weights.astype(bf16), v) + dot(new_weights.astype(bf16), new_v)
    out[:, WIDE:PACK] = stats


def join_kernel(order, prefix, recv, out, wide):
    for h in range(GROUPS):
        wide[4 * h : 4 * h + 4] = recv[h].astype(f32)
    tails = dot(order[...], wide[...].astype(bf16))
    tail_stats = tails[:, WIDE:PACK]
    prefix_stats = prefix[:, WIDE:PACK]
    stats = jnp.zeros((ROWS, 128), f32)
    for head in range(HEADS):
        at = slice(head * HD, (head + 1) * HD)
        left_m, left_l = get_stats(prefix_stats, head)
        right_m, right_l = get_stats(tail_stats, head)
        m = jnp.maximum(left_m, right_m)
        left = jnp.exp(left_m - m)
        right = jnp.exp(right_m - m)
        stats = put_stats(stats, head, m, left * left_l + right * right_l)
        joined = (left * prefix[:, at] + right * tails[:, at]).astype(bf16)
        for n in range(NROW):
            out[n, :, at] = joined
    stats = stats.astype(bf16)
    for n in range(NROW):
        out[n, :, WIDE:PACK] = stats


def columns_of(rows, other):
    return lax.dot_general(
        rows.astype(bf16), other.astype(bf16), (((0,), (0,)), ((), ())), preferred_element_type=f32
    )


def out_kernel(recv, weight, base, out):
    row, lane = iota((16, 128), 0), iota((16, 128), 1)
    head = (row & 7) * 4
    first = jnp.where(row < 8, head, head + 1)
    last = jnp.where(row < 8, head, head + 2)
    chosen = one_hot((lane >= first) & (lane <= last) & ((row & 7) < HEADS))
    tables = [dot_t(chosen, recv[n, :, WIDE:PACK]) for n in range(NROW)]
    m = tables[0][0:8]
    for table in tables[1:]:
        m = jnp.maximum(m, table[0:8])
    scales = [jnp.exp(table[0:8] - m) for table in tables]
    total = scales[0] * tables[0][8:16]
    for n in range(1, NROW):
        total = total + scales[n] * tables[n][8:16]
    spread = iota((16, WIDE), 0) & 7
    spread = one_hot(spread == (iota((16, WIDE), 1) >> 7))
    inverse = jnp.where(iota((8, ROWS), 0) < HEADS, 1.0 / total, 0.0)
    attended = jnp.zeros((ROWS, WIDE), f32)
    for n in range(NROW):
        factor = jnp.concatenate(split(scales[n] * inverse), axis=0)
        attended = attended + columns_of(factor, spread) * recv[n, :, 0:WIDE].astype(f32)
    partial = (dot(attended.astype(bf16), weight[...]) + base[...]).astype(bf16)
    for n in range(NCOL):
        out[n] = partial


def centred(values, gain):
    mean = jnp.mean(values, axis=1, keepdims=True)
    away = values - mean
    return mean, jnp.sum(away * away, axis=1, keepdims=True), (away * gain).astype(bf16)


def as_rows(columns, order=None):
    lane = iota((ROWS, 8), 1)
    table = jnp.zeros((ROWS, 8), f32)
    for at, column in columns:
        table = jnp.where(lane == at, column, table)
    if order is None:
        order = iota((ROWS, ROWS), 1)
    order = one_hot(iota((ROWS, ROWS), 0) == order)
    return lax.dot_general(
        table.astype(bf16), order, (((0,), (0,)), ((), ())), preferred_element_type=f32
    )


def up_kernel(recv, vectors, extra, weight, hidden, out):
    values = recv[0].astype(f32)
    for n in range(1, NCOL):
        values = values + recv[n].astype(f32)
    hidden[...] = values
    mean, spread, scaled = centred(values, vectors[0:1])
    rows = as_rows(list(zip((4, 5, 6, 7), split(mean) + split(spread))))
    rows = jnp.concatenate([rows, jnp.zeros((8, BLOCK - ROWS), f32)], axis=1)
    edge = iota((8, BLOCK), 0)
    for n in range(NROW):
        out[n, 0:ROWS] = dot(scaled, weight[:, n * BLOCK : (n + 1) * BLOCK]).astype(bf16)
        out[n, ROWS : ROWS + 8] = jnp.where(edge < 4, extra[n], rows).astype(bf16)


def projected(recv, bias, edges, gain_at, shift_at, mean_at, spread_at):
    width = recv.shape[2]
    for n in range(NROW):
        edge = recv[n, ROWS : ROWS + 8].astype(f32)
        edges[0, 8 * n : 8 * n + 8] = edge[:, 0:128]
        edges[1, 8 * n : 8 * n + 8, 0 : width - 128] = edge[:, 128:width]

    def row(at):
        halves = [edges[half, pl.ds(at, NROW, stride=8), :] for half in range(2)]
        return jnp.concatenate(halves, axis=1)[:, 0:width]

    means = (row(mean_at) + row(mean_at + 1))[:, 0:ROWS]
    spreads = (row(spread_at) + row(spread_at + 1))[:, 0:ROWS]
    away = means - jnp.mean(means, axis=0, keepdims=True)
    spread = jnp.sum(spreads + BLOCK * away * away, axis=0, keepdims=True)
    scale = lax.rsqrt(spread / D + norm_eps)
    high, low = split(away)
    gains = [row(at) for at in gain_at]
    lefts = [high, low] if len(gains) == 1 else [high, low, high, low]
    rights = [part for part in gains for _ in range(2)]
    fixed = columns_of(jnp.concatenate(lefts, axis=0), jnp.concatenate(rights, axis=0))
    shifted = bias + sum(jnp.sum(row(at), axis=0, keepdims=True) for at in shift_at)
    high, rest = split(scale)
    middle, low = split(rest)
    at = iota((8, ROWS), 0)
    parts = jnp.where(at == 0, high, jnp.where(at == 1, middle, jnp.where(at == 2, low, 0.0)))
    scales = columns_of(parts, jnp.ones((8, width), f32))
    total = recv[0, 0:ROWS].astype(f32)
    for n in range(1, NROW):
        total = total + recv[n, 0:ROWS].astype(f32)
    return (total + fixed) * scales + shifted


def hidden_kernel(recv, vectors, out, edges):
    v = projected(recv, vectors[4:5], edges, (0, 1), (2, 3), 4, 6)
    v = 0.5 * v * (1.0 + jnp.tanh(math.sqrt(2.0 / math.pi) * (v + 0.044715 * (v * v * v))))
    v = v.astype(bf16)
    for n in range(NROW):
        out[n] = v


def down_kernel(recv, weight, vectors, out):
    total = vectors[3:4]
    for n in range(NROW):
        total = total + dot(recv[n], weight[n * BLOCK : (n + 1) * BLOCK])
    total = total.astype(bf16)
    for n in range(NCOL):
        out[n] = total


def next_kernel(recv, hidden, vectors, extra, weight, layer_out, out):
    values = hidden[...]
    for n in range(NCOL):
        values = values + recv[n].astype(f32)
    low = values.astype(bf16)
    values = low.astype(f32)
    layer_out[...] = dot_t(low, own_columns()).astype(bf16)
    mean, spread, scaled = centred(values, vectors[1:2])
    scores = jnp.sum(values * vectors[2:3], axis=1, keepdims=True)
    lane = iota((ROWS, ROWS), 1)
    by_step = ((lane & 31) << 1) + (lane >> 5)
    rows = as_rows(list(zip((2, 3, 4, 5), split(mean) + split(spread))))
    rows = rows + as_rows(list(zip((6, 7), split(scores))), by_step)
    width = out.shape[2]
    rows = jnp.concatenate([rows, jnp.zeros((8, width - ROWS), f32)], axis=1)
    edge = iota((8, width), 0)
    for n in range(NROW):
        out[n, 0:ROWS] = dot(scaled, weight[:, n * width : (n + 1) * width]).astype(bf16)
        out[n, ROWS : ROWS + 8] = jnp.where(edge < 2, extra[n], rows).astype(bf16)


def final_kernel(recv, vectors, projected_next, score_out, wide, edges):
    width = projected_next.shape[2]
    wide[...] = projected(recv, vectors[5:6, 0:width], edges, (0,), (1,), 2, 4)
    for i in range(ROWS // 2):
        projected_next[i] = wide[2 * i : 2 * i + 2].astype(bf16)
    scores = edges[0, pl.ds(6, NROW, stride=8), :] + edges[0, pl.ds(7, NROW, stride=8), :]
    total = jnp.sum(scores, axis=0, keepdims=True)
    half = ROWS // 2
    score_out[0:1] = total[:, 0:half]
    score_out[1:2] = total[:, half:ROWS]


def call(kernel, out, scalars, arrays, scratch=(), remote=(), limit=16, home=pltpu.VMEM):
    many = isinstance(out, list)
    outs = out if many else [out]
    moved = sum(a.size * a.dtype.itemsize for a in arrays)
    moved += sum(math.prod(s) * jnp.dtype(t).itemsize for s, t in outs)
    shapes = [jax.ShapeDtypeStruct(s, t) for s, t in outs]
    vmem = pl.BlockSpec(memory_space=pltpu.VMEM)
    specs = [pl.BlockSpec(memory_space=pltpu.HBM)] * len(remote)
    specs += [pl.BlockSpec(memory_space=pltpu.SMEM)] * len(scalars) + [vmem] * len(arrays)
    return pl.pallas_call(
        kernel,
        out_shape=shapes if many else shapes[0],
        in_specs=specs,
        out_specs=[vmem] * len(outs) if many else pl.BlockSpec(memory_space=home),
        scratch_shapes=scratch,
        cost_estimate=pl.CostEstimate(flops=0, bytes_accessed=moved, transcendentals=0),
        compiler_params=pltpu.CompilerParams(vmem_limit_bytes=limit * 1024 * 1024),
        name=kernel.__name__,
    )(*remote, *scalars, *arrays)


def exchange(x, axis):
    return lax.all_to_all(x, axis, split_axis=0, concat_axis=0, tiled=True)


def shards(
    residual,
    fresh_qkv,
    prefix_pages,
    tail_pages,
    prefix_item,
    tail_item,
    prefix_length,
    tail_length,
    out_weight,
    out_bias,
    mlp_gain,
    mlp_shift,
    up_weight,
    up_bias,
    down_weight,
    down_bias,
    next_gain,
    next_shift,
    score_weight,
    qkv_weight,
    qkv_bias,
):
    cont_local = residual.shape[0]
    share = residual.shape[2]
    width = qkv_bias.shape[0]

    small = jnp.concatenate(
        [
            mlp_gain,
            mlp_shift,
            next_gain,
            next_shift,
            score_weight,
            up_bias,
            qkv_bias,
            out_bias,
            down_bias,
            jnp.zeros((192,), bf16),
        ]
    ).reshape(16, 128)
    stored = jnp.swapaxes(fresh_qkv, 1, 2).reshape(cont_local, 3, 2, WIDE)
    sent = call(
        send_kernel,
        ((GROUPS, KEYROWS + TOK, HD), bf16),
        [],
        [],
        [
            pltpu.VMEM((4, 128), jnp.int32),
            pltpu.VMEM((cont_local, 2, WIDE), bf16),
            pltpu.VMEM((ROWS, WIDE), f32),
            pltpu.VMEM((GROUPS * TOK, HD), f32),
            pltpu.VMEM((GROUPS, KEYROWS + TOK, HD), bf16),
            pltpu.SemaphoreType.DMA((2 + 2 * HEADS,)),
            pltpu.SemaphoreType.DMA((1 + 2 * HEADS,)),
        ],
        [tail_item.reshape(4, 128), stored, prefix_pages],
        60,
        pltpu.HBM,
    )
    arrived = exchange(sent, "pages")
    tail_offset, prefix_offset, order, base, vectors = call(
        ready_kernel,
        [
            ((ROWS, 8 * TOK), f32),
            ((ROWS, GROUPS * TOK), f32),
            ((ROWS, ROWS), bf16),
            ((ROWS, BLOCK), f32),
            ((8, BLOCK), f32),
        ],
        [tail_item, tail_length, prefix_item, prefix_length],
        [residual.reshape(ROWS, share), small],
    )
    tails = call(
        tail_kernel,
        ((GROUPS, 4, PACK), bf16),
        [],
        [arrived, tail_pages, tail_offset],
        [pltpu.VMEM((HEADS, ROWS, HD), f32), pltpu.VMEM((ROWS, PACK), f32)],
    )
    tails = exchange(tails, "pages")
    prefix, up_rows, qkv_rows = call(
        prefix_kernel,
        [((ROWS, PACK), f32), ((NROW, 8, BLOCK), f32), ((NROW, 8, width), f32)],
        [],
        [
            fresh_qkv.reshape(ROWS, 3 * WIDE),
            arrived,
            prefix_offset,
            vectors,
            up_weight,
            qkv_weight,
        ],
    )
    joined = call(
        join_kernel,
        ((NROW, ROWS, PACK), bf16),
        [],
        [order, prefix, tails],
        [pltpu.VMEM((ROWS, PACK), f32)],
    )
    joined = exchange(joined, "row")
    partial = call(
        out_kernel,
        ((NCOL, ROWS, BLOCK), bf16),
        [],
        [joined, out_weight, base],
    )
    partial = exchange(partial, "col")
    hidden_one, partial = call(
        up_kernel,
        [((ROWS, BLOCK), f32), ((NROW, ROWS + 8, BLOCK), bf16)],
        [],
        [partial, vectors, up_rows, up_weight],
    )
    partial = exchange(partial, "row")
    hidden_two = call(
        hidden_kernel,
        ((NROW, ROWS, BLOCK), bf16),
        [],
        [partial, vectors],
        [pltpu.VMEM((2, ROWS, 128), f32)],
    )
    hidden_two = exchange(hidden_two, "row")
    partial = call(
        down_kernel, ((NCOL, ROWS, BLOCK), bf16), [], [hidden_two, down_weight, vectors]
    )
    partial = exchange(partial, "col")
    layer_out, partial = call(
        next_kernel,
        [((ROWS, share), bf16), ((NROW, ROWS + 8, width), bf16)],
        [],
        [partial, hidden_one, vectors, qkv_rows, qkv_weight],
    )
    partial = exchange(partial, "row")
    projected_next, score_sum = call(
        final_kernel,
        [((cont_local, 2, width), bf16), ((2, cont_local), f32)],
        [],
        [partial, vectors],
        [pltpu.VMEM((ROWS, width), f32), pltpu.VMEM((2, ROWS, 128), f32)],
    )
    return (layer_out.reshape(cont_local, 2, share), score_sum.T, projected_next)


def solution(mesh):
    in_specs = (
        P("pages", None, ("row", "col")),
        P("pages", None, None, "col"),
        P("pages", None, "row", "col"),
        P("pages", None, "row", "col"),
        P(),
        P(),
        P(),
        P(),
        P("col", "row"),
        P(("row", "col")),
        P("row"),
        P("row"),
        P("row", "col"),
        P(("col", "row")),
        P("col", "row"),
        P(("row", "col")),
        P("row"),
        P("row"),
        P("row"),
        P("row", "col"),
        P(("col", "row")),
    )
    out_specs = (
        P("pages", None, ("row", "col")),
        P("pages", None),
        P("pages", None, ("col", "row")),
    )
    return jax.shard_map(shards, mesh=mesh, in_specs=in_specs, out_specs=out_specs, check_vma=False)
```

```python
import math

import jax
import jax.numpy as jnp
from jax import lax
from jax.experimental import pallas as pl
from jax.experimental.pallas import tpu as pltpu
from jax.sharding import PartitionSpec as P

D = 2048
H = 16
HD = 128
PAGE = 128
MAXPAGES = 8
CONT = 16

GROUPS = 16
NROW = 8
NCOL = 4
ROWS = 64
HEADS = 4
WIDE = HEADS * HD
PACK = WIDE + 128
BLOCK = D // NROW
TOK = 16
TAILS = 32
KEYROWS = 2 * HEADS * TOK

masked_score = -1e30
norm_eps = 1e-05
f32 = jnp.float32
bf16 = jnp.bfloat16


def dot(a, b):
    return jnp.dot(a, b, preferred_element_type=f32)


def dot_t(a, b):
    return lax.dot_general(a, b, (((1,), (1,)), ((), ())), preferred_element_type=f32)


def iota(shape, dim):
    return lax.broadcasted_iota(jnp.int32, shape, dim)


def one_hot(mask):
    return jnp.where(mask, 1.0, 0.0).astype(bf16)


def rounded(x):
    return x.astype(bf16).astype(f32)


def slope_of(head):
    return jnp.exp2(jnp.full((ROWS, 1), -8.0 / H, f32) * (head + 1).astype(f32))


def put_stats(stats, head, m, l):
    lane = iota((ROWS, 128), 1)
    hi = rounded(l)
    stats = jnp.where(lane == head * 4, m, stats)
    stats = jnp.where(lane == head * 4 + 1, hi, stats)
    return jnp.where(lane == head * 4 + 2, l - hi, stats)


def send_kernel(tail_item, fresh, pages, out, items, query, wide, rows, stage, sems, out_sems):
    copies = [
        pltpu.make_async_copy(tail_item, items, sems.at[0]),
        pltpu.make_async_copy(fresh.at[:, 0], query, sems.at[1]),
    ]
    for n in range(2 * HEADS):
        head = slice((n % HEADS) * HD, (n % HEADS + 1) * HD)
        copies.append(
            pltpu.make_async_copy(
                pages.at[:, n // HEADS, :, head],
                stage.at[:, n * TOK : (n + 1) * TOK],
                sems.at[2 + n],
            )
        )
    for copy in copies:
        copy.start()
    group = lax.axis_index("pages")
    source, lane = iota((128, ROWS), 0), iota((128, ROWS), 1)
    place = (((lane >> 2) & 3) == (source >> 5)) & (
        (source & (TAILS - 1)) == group * 2 + ((lane >> 1) & 1)
    )
    place = one_hot(place)
    copies[0].wait()
    local = (items[...] & (TAILS - 1)).astype(f32).astype(bf16)
    found = dot(local, place)
    here = iota(found.shape, 0) == (iota(found.shape, 1) >> 4)
    target = jnp.sum(jnp.where(here, found, 0.0), axis=0, keepdims=True).astype(jnp.int32) * 2
    target = target + (iota((1, ROWS), 1) & 1)
    pick = one_hot(iota((ROWS, ROWS), 0) == target)
    copies[1].wait()
    for j in range(TAILS):
        wide[2 * j : 2 * j + 2] = query[j].astype(f32)
    leaving = []
    for n in range(2 * HEADS):
        part = slice(n * TOK, (n + 1) * TOK)
        copies[2 + n].wait()
        leaving.append(pltpu.make_async_copy(stage.at[:, part], out.at[:, part], out_sems.at[n]))
        leaving[n].start()
    picked = lax.dot_general(
        pick, wide[...].astype(bf16), (((0,), (0,)), ((), ())), preferred_element_type=f32
    )
    for h in range(GROUPS):
        for head in range(HEADS):
            at = h * TOK + head * 4
            rows[at : at + 4] = picked[4 * h : 4 * h + 4, head * HD : (head + 1) * HD]
    stage[:, KEYROWS:] = rows[...].reshape(GROUPS, TOK, HD).astype(bf16)
    last = pltpu.make_async_copy(
        stage.at[:, KEYROWS : KEYROWS + TOK],
        out.at[:, KEYROWS : KEYROWS + TOK],
        out_sems.at[2 * HEADS],
    )
    last.start()
    for copy in leaving + [last]:
        copy.wait()


def own_columns():
    share = BLOCK // NCOL
    first = lax.axis_index("col") * share
    return one_hot(iota((share, BLOCK), 1) == iota((share, BLOCK), 0) + first)


def gain_rows(gain, shift):
    row = iota((16, BLOCK), 0)
    return jnp.where(row == 0, gain, jnp.where(row == 1, shift, 0.0)).astype(bf16)


def split(x):
    hi = rounded(x)
    return hi, x - hi


def ready_kernel(
    tail_item,
    tail_length,
    prefix_item,
    prefix_length,
    residual,
    small,
    tail_offset,
    prefix_offset,
    order,
    base,
    vectors,
):
    group = lax.axis_index("pages")
    row_index = lax.axis_index("row")
    row = iota((ROWS, 1), 0)
    step = row & 1
    lens = jnp.zeros((ROWS, 1), jnp.int32)
    own_lens = jnp.zeros((ROWS, 1), jnp.int32)
    lane = iota((1, ROWS), 1)
    target = lane & 1
    for j in range(TAILS):
        here = (row >> 1) == j
        lens = jnp.where(here, tail_length[tail_item[group * TAILS + j]], lens)
        own_lens = jnp.where(here, tail_length[group * TAILS + j], own_lens)
        item = tail_item[(j // 2) * TAILS + group * 2 + j % 2] - group * TAILS
        target = target + jnp.where((lane >> 1) == j, item * 2, 0)
    order[...] = one_hot(iota((ROWS, ROWS), 0) == target)

    key = iota((ROWS, 8 * TOK), 1)
    token = (key & (TOK - 1)) + row_index * TOK
    usable = ((key >> 4) == ((row >> 1) & 7)) & (token < lens)
    offset = (token - lens - step).astype(f32)
    tail_offset[...] = jnp.where(usable, offset, masked_score)

    row_prompt = row >> 5
    prompt_lens = jnp.where(
        row_prompt == 0, prefix_length[group * 2], prefix_length[group * 2 + 1]
    )
    query_pos = prompt_lens + own_lens + step
    lane = iota((1, GROUPS * TOK), 1)
    key_pos = (lane & (TOK - 1)) + row_index * TOK
    key_prompt = jnp.zeros((1, GROUPS * TOK), jnp.int32)
    for h in range(GROUPS):
        item = prefix_item[h * GROUPS + group]
        here = (lane >> 4) == h
        key_pos = key_pos + jnp.where(here, (item & (MAXPAGES - 1)) * PAGE, 0)
        key_prompt = jnp.where(here, (item >> 3) - group * 2, key_prompt)
    usable = (key_prompt == row_prompt) & (key_pos < prompt_lens)
    offset = (key_pos - query_pos).astype(f32)
    prefix_offset[...] = jnp.where(usable, offset, masked_score)

    table = small[...].astype(f32)

    def line(at):
        return jnp.concatenate([table[at : at + 1], table[at + 1 : at + 2]], axis=1)

    share = BLOCK // NCOL
    place = own_columns()

    def placed(values):
        return dot(jnp.broadcast_to(values, (8, share)).astype(bf16), place)[0:1]

    base[...] = dot(residual[...], place) + placed(table[13:14, 64:128])
    rows = [line(0), line(4), line(8), placed(table[14:15, 0:64]), line(10), line(12), line(2), line(6)]
    edge = iota((8, BLOCK), 0)
    filled = jnp.zeros((8, BLOCK), f32)
    for at, values in enumerate(rows):
        filled = jnp.where(edge == at, values, filled)
    vectors[...] = filled


def tail_kernel(recv, tails, distance, out, query, wide):
    first_head = lax.axis_index("col") * HEADS
    distance = distance[...]
    usable = distance > 0.5 * masked_score
    for g in range(GROUPS):
        rows = recv[g, KEYROWS:].astype(f32)
        for head in range(HEADS):
            query[head, 4 * g : 4 * g + 4] = rows[4 * head : 4 * head + 4]
    some = ROWS * 8 // TAILS
    blocks = ROWS // some
    stats = jnp.zeros((ROWS, 128), f32)
    scores, weights = [], []
    for head in range(HEADS):
        at = slice(head * HD, (head + 1) * HD)
        q = query[head].astype(bf16)
        parts = []
        for n in range(blocks):
            k = tails[8 * n : 8 * n + 8, 0, :, at].reshape(8 * TOK, HD)
            parts.append(dot_t(q[n * some : (n + 1) * some], k))
        scores.append(jnp.concatenate(parts, axis=0))
    for head in range(HEADS):
        biased = scores[head] * (1.0 / math.sqrt(HD)) + slope_of(first_head + head) * distance
        biased = jnp.where(usable, biased, masked_score)
        m = rounded(jnp.max(biased, axis=1, keepdims=True))
        shares = jnp.where(usable, jnp.exp(biased - m), 0.0)
        stats = put_stats(stats, head, m, jnp.sum(shares, axis=1, keepdims=True))
        weights.append(shares.astype(bf16))
    for head in range(HEADS):
        at = slice(head * HD, (head + 1) * HD)
        for n in range(blocks):
            v = tails[8 * n : 8 * n + 8, 1, :, at].reshape(8 * TOK, HD)
            rows = slice(n * some, (n + 1) * some)
            wide[rows, at] = dot(weights[head][rows], v)
    wide[:, WIDE:PACK] = stats
    for g in range(GROUPS):
        out[g] = wide[4 * g : 4 * g + 4].astype(bf16)


def prefix_kernel(
    fresh, recv, distance, vectors, up_weight, qkv_weight, out, up_rows, qkv_rows
):
    both = gain_rows(vectors[0:1], vectors[6:7])
    edge = iota((8, BLOCK), 0)
    for n in range(NROW):
        parts = dot(both, up_weight[:, n * BLOCK : (n + 1) * BLOCK])
        rows = jnp.zeros((8, BLOCK), f32)
        for at, values in enumerate(split(parts[0:1]) + split(parts[1:2])):
            rows = jnp.where(edge == at, values, rows)
        up_rows[n] = rows
    both = gain_rows(vectors[1:2], vectors[7:8])
    width = qkv_rows.shape[2]
    for n in range(NROW):
        qkv_rows[n] = dot(both, qkv_weight[:, n * width : (n + 1) * width])[0:8]

    distance = distance[...]
    usable = distance > 0.5 * masked_score
    row_index = lax.axis_index("row")
    first_head = lax.axis_index("col") * HEADS
    row = iota((ROWS, 1), 0)
    keys = GROUPS * TOK
    col = iota((ROWS, ROWS), 1)
    new_usable = ((col >> 1) == (row >> 1)) & ((col & 1) <= (row & 1)) & (row_index == 0)
    new_offset = ((col & 1) - (row & 1)).astype(f32)
    stats = jnp.zeros((ROWS, 128), f32)
    for head in range(HEADS):
        at = slice(head * HD, (head + 1) * HD)
        q = fresh[:, head * HD : (head + 1) * HD]
        new_k = fresh[:, WIDE + head * HD : WIDE + (head + 1) * HD]
        new_v = fresh[:, 2 * WIDE + head * HD : 2 * WIDE + (head + 1) * HD]
        k = recv[:, head * TOK : (head + 1) * TOK].reshape(keys, HD)
        v = recv[:, (HEADS + head) * TOK : (HEADS + head + 1) * TOK].reshape(keys, HD)
        slope = slope_of(first_head + head)
        scores = dot_t(q, k) * (1.0 / math.sqrt(HD)) + slope * distance
        scores = jnp.where(usable, scores, masked_score)
        new_scores = dot_t(q, new_k) * (1.0 / math.sqrt(HD)) + slope * new_offset
        new_scores = jnp.where(new_usable, new_scores, masked_score)
        m = rounded(
            jnp.maximum(
                jnp.max(scores, axis=1, keepdims=True),
                jnp.max(new_scores, axis=1, keepdims=True),
            )
        )
        weights = jnp.where(usable, jnp.exp(scores - m), 0.0)
        new_weights = jnp.where(new_usable, jnp.exp(new_scores - m), 0.0)
        total = jnp.sum(weights, axis=1, keepdims=True) + jnp.sum(
            new_weights, axis=1, keepdims=True
        )
        stats = put_stats(stats, head, m, total)
        out[:, at] = dot(weights.astype(bf16), v) + dot(new_weights.astype(bf16), new_v)
    out[:, WIDE:PACK] = stats


def columns_of(rows, other):
    return lax.dot_general(
        rows.astype(bf16), other.astype(bf16), (((0,), (0,)), ((), ())), preferred_element_type=f32
    )


def head_spread():
    return one_hot((iota((16, WIDE), 0) & 7) == (iota((16, WIDE), 1) >> 7))


def join_kernel(order, prefix, recv, out, wide):
    for h in range(GROUPS):
        wide[4 * h : 4 * h + 4] = recv[h].astype(f32)
    row, lane = iota((16, 128), 0), iota((16, 128), 1)
    head = (row & 7) * 4
    first = jnp.where(row < 8, head, head + 1)
    last = jnp.where(row < 8, head, head + 2)
    chosen = one_hot((lane >= first) & (lane <= last) & ((row & 7) < HEADS))
    left = dot_t(chosen, prefix[:, WIDE:PACK].astype(bf16))
    tails = dot(order[...], wide[...].astype(bf16))
    right = dot_t(chosen, tails[:, WIDE:PACK].astype(bf16))
    m = jnp.maximum(left[0:8], right[0:8])
    left_scale = jnp.exp(left[0:8] - m)
    right_scale = jnp.exp(right[0:8] - m)
    total = split(left_scale * left[8:16] + right_scale * right[8:16])
    spread = head_spread()
    left_scale = columns_of(jnp.concatenate(split(left_scale), axis=0), spread)
    right_scale = columns_of(jnp.concatenate(split(right_scale), axis=0), spread)
    joined = (left_scale * prefix[:, 0:WIDE] + right_scale * tails[:, 0:WIDE]).astype(bf16)
    blank = jnp.zeros((8, 128 - ROWS), f32)
    parts = []
    for part in (m,) + total:
        parts = parts + [part, blank]
    stats = jnp.concatenate(parts, axis=1).astype(bf16)
    for n in range(NROW):
        out[n, 0:ROWS] = joined
        out[n, ROWS : ROWS + 8, 0:384] = stats
        out[n, ROWS : ROWS + 8, 384:WIDE] = jnp.zeros((8, WIDE - 384), bf16)


def out_kernel(recv, weight, base, out):
    tables = [recv[n, ROWS : ROWS + 8, 0:384].astype(f32) for n in range(NROW)]
    maxima = [table[:, 0:ROWS] for table in tables]
    m = maxima[0]
    for part in maxima[1:]:
        m = jnp.maximum(m, part)
    scales = [jnp.exp(part - m) for part in maxima]
    sums = [table[:, 128 : 128 + ROWS] + table[:, 256 : 256 + ROWS] for table in tables]
    total = scales[0] * sums[0]
    for n in range(1, NROW):
        total = total + scales[n] * sums[n]
    spread = head_spread()
    inverse = jnp.where(iota((8, ROWS), 0) < HEADS, 1.0 / total, 0.0)
    attended = jnp.zeros((ROWS, WIDE), f32)
    for n in range(NROW):
        factor = jnp.concatenate(split(scales[n] * inverse), axis=0)
        attended = attended + columns_of(factor, spread) * recv[n, 0:ROWS].astype(f32)
    partial = (dot(attended.astype(bf16), weight[...]) + base[...]).astype(bf16)
    for n in range(NCOL):
        out[n] = partial


def centred(values, gain):
    mean = jnp.mean(values, axis=1, keepdims=True)
    away = values - mean
    return mean, jnp.sum(away * away, axis=1, keepdims=True), (away * gain).astype(bf16)


def as_rows(columns, order=None):
    lane = iota((ROWS, 8), 1)
    table = jnp.zeros((ROWS, 8), f32)
    for at, column in columns:
        table = jnp.where(lane == at, column, table)
    if order is None:
        order = iota((ROWS, ROWS), 1)
    order = one_hot(iota((ROWS, ROWS), 0) == order)
    return lax.dot_general(
        table.astype(bf16), order, (((0,), (0,)), ((), ())), preferred_element_type=f32
    )


def up_kernel(recv, vectors, extra, weight, hidden, out):
    values = recv[0].astype(f32)
    for n in range(1, NCOL):
        values = values + recv[n].astype(f32)
    hidden[...] = values
    mean, spread, scaled = centred(values, vectors[0:1])
    rows = as_rows(list(zip((4, 5, 6, 7), split(mean) + split(spread))))
    rows = jnp.concatenate([rows, jnp.zeros((8, BLOCK - ROWS), f32)], axis=1)
    edge = iota((8, BLOCK), 0)
    for n in range(NROW):
        out[n, 0:ROWS] = dot(scaled, weight[:, n * BLOCK : (n + 1) * BLOCK]).astype(bf16)
        out[n, ROWS : ROWS + 8] = jnp.where(edge < 4, extra[n], rows).astype(bf16)


def projected(recv, bias, edges, gain_at, shift_at, mean_at, spread_at):
    width = recv.shape[2]
    for n in range(NROW):
        edge = recv[n, ROWS : ROWS + 8].astype(f32)
        edges[0, 8 * n : 8 * n + 8] = edge[:, 0:128]
        edges[1, 8 * n : 8 * n + 8, 0 : width - 128] = edge[:, 128:width]

    def row(at):
        halves = [edges[half, pl.ds(at, NROW, stride=8), :] for half in range(2)]
        return jnp.concatenate(halves, axis=1)[:, 0:width]

    means = (row(mean_at) + row(mean_at + 1))[:, 0:ROWS]
    spreads = (row(spread_at) + row(spread_at + 1))[:, 0:ROWS]
    away = means - jnp.mean(means, axis=0, keepdims=True)
    spread = jnp.sum(spreads + BLOCK * away * away, axis=0, keepdims=True)
    scale = lax.rsqrt(spread / D + norm_eps)
    high, low = split(away)
    gains = [row(at) for at in gain_at]
    lefts = [high, low] if len(gains) == 1 else [high, low, high, low]
    rights = [part for part in gains for _ in range(2)]
    fixed = columns_of(jnp.concatenate(lefts, axis=0), jnp.concatenate(rights, axis=0))
    shifted = bias + sum(jnp.sum(row(at), axis=0, keepdims=True) for at in shift_at)
    high, rest = split(scale)
    middle, low = split(rest)
    at = iota((8, ROWS), 0)
    parts = jnp.where(at == 0, high, jnp.where(at == 1, middle, jnp.where(at == 2, low, 0.0)))
    scales = columns_of(parts, jnp.ones((8, width), f32))
    total = recv[0, 0:ROWS].astype(f32)
    for n in range(1, NROW):
        total = total + recv[n, 0:ROWS].astype(f32)
    return (total + fixed) * scales + shifted


def hidden_kernel(recv, vectors, out, edges):
    v = projected(recv, vectors[4:5], edges, (0, 1), (2, 3), 4, 6)
    v = 0.5 * v * (1.0 + jnp.tanh(math.sqrt(2.0 / math.pi) * (v + 0.044715 * (v * v * v))))
    v = v.astype(bf16)
    for n in range(NROW):
        out[n] = v


def down_kernel(recv, weight, vectors, out):
    total = vectors[3:4]
    for n in range(NROW):
        total = total + dot(recv[n], weight[n * BLOCK : (n + 1) * BLOCK])
    total = total.astype(bf16)
    for n in range(NCOL):
        out[n] = total


def next_kernel(recv, hidden, vectors, extra, weight, layer_out, out):
    values = hidden[...]
    for n in range(NCOL):
        values = values + recv[n].astype(f32)
    low = values.astype(bf16)
    values = low.astype(f32)
    layer_out[...] = dot_t(low, own_columns()).astype(bf16)
    mean, spread, scaled = centred(values, vectors[1:2])
    scores = jnp.sum(values * vectors[2:3], axis=1, keepdims=True)
    lane = iota((ROWS, ROWS), 1)
    by_step = ((lane & 31) << 1) + (lane >> 5)
    rows = as_rows(list(zip((2, 3, 4, 5), split(mean) + split(spread))))
    rows = rows + as_rows(list(zip((6, 7), split(scores))), by_step)
    width = out.shape[2]
    rows = jnp.concatenate([rows, jnp.zeros((8, width - ROWS), f32)], axis=1)
    edge = iota((8, width), 0)
    for n in range(NROW):
        out[n, 0:ROWS] = dot(scaled, weight[:, n * width : (n + 1) * width]).astype(bf16)
        out[n, ROWS : ROWS + 8] = jnp.where(edge < 2, extra[n], rows).astype(bf16)


def final_kernel(recv, vectors, projected_next, score_out, wide, edges):
    width = projected_next.shape[2]
    wide[...] = projected(recv, vectors[5:6, 0:width], edges, (0,), (1,), 2, 4)
    for i in range(ROWS // 2):
        projected_next[i] = wide[2 * i : 2 * i + 2].astype(bf16)
    scores = edges[0, pl.ds(6, NROW, stride=8), :] + edges[0, pl.ds(7, NROW, stride=8), :]
    total = jnp.sum(scores, axis=0, keepdims=True)
    half = ROWS // 2
    score_out[0:1] = total[:, 0:half]
    score_out[1:2] = total[:, half:ROWS]


def call(kernel, out, scalars, arrays, scratch=(), remote=(), limit=16, home=pltpu.VMEM):
    many = isinstance(out, list)
    outs = out if many else [out]
    moved = sum(a.size * a.dtype.itemsize for a in arrays)
    moved += sum(math.prod(s) * jnp.dtype(t).itemsize for s, t in outs)
    shapes = [jax.ShapeDtypeStruct(s, t) for s, t in outs]
    vmem = pl.BlockSpec(memory_space=pltpu.VMEM)
    specs = [pl.BlockSpec(memory_space=pltpu.HBM)] * len(remote)
    specs += [pl.BlockSpec(memory_space=pltpu.SMEM)] * len(scalars) + [vmem] * len(arrays)
    return pl.pallas_call(
        kernel,
        out_shape=shapes if many else shapes[0],
        in_specs=specs,
        out_specs=[vmem] * len(outs) if many else pl.BlockSpec(memory_space=home),
        scratch_shapes=scratch,
        cost_estimate=pl.CostEstimate(flops=0, bytes_accessed=moved, transcendentals=0),
        compiler_params=pltpu.CompilerParams(vmem_limit_bytes=limit * 1024 * 1024),
        name=kernel.__name__,
    )(*remote, *scalars, *arrays)


def exchange(x, axis):
    return lax.all_to_all(x, axis, split_axis=0, concat_axis=0, tiled=True)


def shards(
    residual,
    fresh_qkv,
    prefix_pages,
    tail_pages,
    prefix_item,
    tail_item,
    prefix_length,
    tail_length,
    out_weight,
    out_bias,
    mlp_gain,
    mlp_shift,
    up_weight,
    up_bias,
    down_weight,
    down_bias,
    next_gain,
    next_shift,
    score_weight,
    qkv_weight,
    qkv_bias,
):
    cont_local = residual.shape[0]
    share = residual.shape[2]
    width = qkv_bias.shape[0]

    small = jnp.concatenate(
        [
            mlp_gain,
            mlp_shift,
            next_gain,
            next_shift,
            score_weight,
            up_bias,
            qkv_bias,
            out_bias,
            down_bias,
            jnp.zeros((192,), bf16),
        ]
    ).reshape(16, 128)
    stored = jnp.swapaxes(fresh_qkv, 1, 2).reshape(cont_local, 3, 2, WIDE)
    sent = call(
        send_kernel,
        ((GROUPS, KEYROWS + TOK, HD), bf16),
        [],
        [],
        [
            pltpu.VMEM((4, 128), jnp.int32),
            pltpu.VMEM((cont_local, 2, WIDE), bf16),
            pltpu.VMEM((ROWS, WIDE), f32),
            pltpu.VMEM((GROUPS * TOK, HD), f32),
            pltpu.VMEM((GROUPS, KEYROWS + TOK, HD), bf16),
            pltpu.SemaphoreType.DMA((2 + 2 * HEADS,)),
            pltpu.SemaphoreType.DMA((1 + 2 * HEADS,)),
        ],
        [tail_item.reshape(4, 128), stored, prefix_pages],
        60,
        pltpu.HBM,
    )
    arrived = exchange(sent, "pages")
    tail_offset, prefix_offset, order, base, vectors = call(
        ready_kernel,
        [
            ((ROWS, 8 * TOK), f32),
            ((ROWS, GROUPS * TOK), f32),
            ((ROWS, ROWS), bf16),
            ((ROWS, BLOCK), f32),
            ((8, BLOCK), f32),
        ],
        [tail_item, tail_length, prefix_item, prefix_length],
        [residual.reshape(ROWS, share), small],
    )
    tails = call(
        tail_kernel,
        ((GROUPS, 4, PACK), bf16),
        [],
        [arrived, tail_pages, tail_offset],
        [pltpu.VMEM((HEADS, ROWS, HD), f32), pltpu.VMEM((ROWS, PACK), f32)],
    )
    tails = exchange(tails, "pages")
    prefix, up_rows, qkv_rows = call(
        prefix_kernel,
        [((ROWS, PACK), f32), ((NROW, 8, BLOCK), f32), ((NROW, 8, width), f32)],
        [],
        [
            fresh_qkv.reshape(ROWS, 3 * WIDE),
            arrived,
            prefix_offset,
            vectors,
            up_weight,
            qkv_weight,
        ],
    )
    joined = call(
        join_kernel,
        ((NROW, ROWS + 8, WIDE), bf16),
        [],
        [order, prefix, tails],
        [pltpu.VMEM((ROWS, PACK), f32)],
    )
    joined = exchange(joined, "row")
    partial = call(
        out_kernel,
        ((NCOL, ROWS, BLOCK), bf16),
        [],
        [joined, out_weight, base],
    )
    partial = exchange(partial, "col")
    hidden_one, partial = call(
        up_kernel,
        [((ROWS, BLOCK), f32), ((NROW, ROWS + 8, BLOCK), bf16)],
        [],
        [partial, vectors, up_rows, up_weight],
    )
    partial = exchange(partial, "row")
    hidden_two = call(
        hidden_kernel,
        ((NROW, ROWS, BLOCK), bf16),
        [],
        [partial, vectors],
        [pltpu.VMEM((2, ROWS, 128), f32)],
    )
    hidden_two = exchange(hidden_two, "row")
    partial = call(
        down_kernel, ((NCOL, ROWS, BLOCK), bf16), [], [hidden_two, down_weight, vectors]
    )
    partial = exchange(partial, "col")
    layer_out, partial = call(
        next_kernel,
        [((ROWS, share), bf16), ((NROW, ROWS + 8, width), bf16)],
        [],
        [partial, hidden_one, vectors, qkv_rows, qkv_weight],
    )
    partial = exchange(partial, "row")
    projected_next, score_sum = call(
        final_kernel,
        [((cont_local, 2, width), bf16), ((2, cont_local), f32)],
        [],
        [partial, vectors],
        [pltpu.VMEM((ROWS, width), f32), pltpu.VMEM((2, ROWS, 128), f32)],
    )
    return (layer_out.reshape(cont_local, 2, share), score_sum.T, projected_next)


def solution(mesh):
    in_specs = (
        P("pages", None, ("row", "col")),
        P("pages", None, None, "col"),
        P("pages", None, "row", "col"),
        P("pages", None, "row", "col"),
        P(),
        P(),
        P(),
        P(),
        P("col", "row"),
        P(("row", "col")),
        P("row"),
        P("row"),
        P("row", "col"),
        P(("col", "row")),
        P("col", "row"),
        P(("row", "col")),
        P("row"),
        P("row"),
        P("row"),
        P("row", "col"),
        P(("col", "row")),
    )
    out_specs = (
        P("pages", None, ("row", "col")),
        P("pages", None),
        P("pages", None, ("col", "row")),
    )
    return jax.shard_map(shards, mesh=mesh, in_specs=in_specs, out_specs=out_specs, check_vma=False)
```

```python
import math

import jax
import jax.numpy as jnp
from jax import lax
from jax.experimental import pallas as pl
from jax.experimental.pallas import tpu as pltpu
from jax.sharding import PartitionSpec as P

D = 2048
H = 16
HD = 128
PAGE = 128
MAXPAGES = 8
CONT = 16

GROUPS = 16
NROW = 8
NCOL = 4
ROWS = 64
HEADS = 4
WIDE = HEADS * HD
PACK = WIDE + 128
BLOCK = D // NROW
TOK = 16
TAILS = 32
KEYROWS = 2 * HEADS * TOK

masked_score = -1e30
norm_eps = 1e-05
f32 = jnp.float32
bf16 = jnp.bfloat16


def dot(a, b):
    return jnp.dot(a, b, preferred_element_type=f32)


def dot_t(a, b):
    return lax.dot_general(a, b, (((1,), (1,)), ((), ())), preferred_element_type=f32)


def iota(shape, dim):
    return lax.broadcasted_iota(jnp.int32, shape, dim)


def one_hot(mask):
    return jnp.where(mask, 1.0, 0.0).astype(bf16)


def rounded(x):
    return x.astype(bf16).astype(f32)


def slope_of(head):
    return jnp.exp2(jnp.full((ROWS, 1), -8.0 / H, f32) * (head + 1).astype(f32))


def put_stats(stats, head, m, l):
    lane = iota((ROWS, 128), 1)
    hi = rounded(l)
    stats = jnp.where(lane == head * 4, m, stats)
    stats = jnp.where(lane == head * 4 + 1, hi, stats)
    return jnp.where(lane == head * 4 + 2, l - hi, stats)


def send_kernel(tail_item, fresh, pages, out, items, query, wide, rows, stage, sems, out_sems):
    copies = [
        pltpu.make_async_copy(tail_item, items, sems.at[0]),
        pltpu.make_async_copy(fresh.at[:, 0], query, sems.at[1]),
    ]
    for n in range(2 * HEADS):
        head = slice((n % HEADS) * HD, (n % HEADS + 1) * HD)
        copies.append(
            pltpu.make_async_copy(
                pages.at[:, n // HEADS, :, head],
                stage.at[:, n * TOK : (n + 1) * TOK],
                sems.at[2 + n],
            )
        )
    for copy in copies:
        copy.start()
    group = lax.axis_index("pages")
    source, lane = iota((128, ROWS), 0), iota((128, ROWS), 1)
    place = (((lane >> 2) & 3) == (source >> 5)) & (
        (source & (TAILS - 1)) == group * 2 + ((lane >> 1) & 1)
    )
    place = one_hot(place)
    copies[0].wait()
    local = (items[...] & (TAILS - 1)).astype(f32).astype(bf16)
    found = dot(local, place)
    here = iota(found.shape, 0) == (iota(found.shape, 1) >> 4)
    target = jnp.sum(jnp.where(here, found, 0.0), axis=0, keepdims=True).astype(jnp.int32) * 2
    target = target + (iota((1, ROWS), 1) & 1)
    pick = one_hot(iota((ROWS, ROWS), 0) == target)
    copies[1].wait()
    for j in range(TAILS):
        wide[2 * j : 2 * j + 2] = query[j].astype(f32)
    leaving = []
    for n in range(2 * HEADS):
        part = slice(n * TOK, (n + 1) * TOK)
        copies[2 + n].wait()
        leaving.append(pltpu.make_async_copy(stage.at[:, part], out.at[:, part], out_sems.at[n]))
        leaving[n].start()
    picked = lax.dot_general(
        pick, wide[...].astype(bf16), (((0,), (0,)), ((), ())), preferred_element_type=f32
    )
    for h in range(GROUPS):
        for head in range(HEADS):
            at = h * TOK + head * 4
            rows[at : at + 4] = picked[4 * h : 4 * h + 4, head * HD : (head + 1) * HD]
    stage[:, KEYROWS:] = rows[...].reshape(GROUPS, TOK, HD).astype(bf16)
    last = pltpu.make_async_copy(
        stage.at[:, KEYROWS : KEYROWS + TOK],
        out.at[:, KEYROWS : KEYROWS + TOK],
        out_sems.at[2 * HEADS],
    )
    last.start()
    for copy in leaving + [last]:
        copy.wait()


def own_columns():
    share = BLOCK // NCOL
    first = lax.axis_index("col") * share
    return one_hot(iota((share, BLOCK), 1) == iota((share, BLOCK), 0) + first)


def gain_rows(gain, shift):
    row = iota((16, BLOCK), 0)
    return jnp.where(row == 0, gain, jnp.where(row == 1, shift, 0.0)).astype(bf16)


def split(x):
    hi = rounded(x)
    return hi, x - hi


def ready_kernel(
    tail_item,
    tail_length,
    prefix_item,
    prefix_length,
    residual,
    small,
    tail_offset,
    prefix_offset,
    order,
    base,
    vectors,
):
    group = lax.axis_index("pages")
    row_index = lax.axis_index("row")
    row = iota((ROWS, 1), 0)
    step = row & 1
    lens = jnp.zeros((ROWS, 1), jnp.int32)
    own_lens = jnp.zeros((ROWS, 1), jnp.int32)
    lane = iota((1, ROWS), 1)
    target = lane & 1
    for j in range(TAILS):
        here = (row >> 1) == j
        lens = jnp.where(here, tail_length[tail_item[group * TAILS + j]], lens)
        own_lens = jnp.where(here, tail_length[group * TAILS + j], own_lens)
        item = tail_item[(j // 2) * TAILS + group * 2 + j % 2] - group * TAILS
        target = target + jnp.where((lane >> 1) == j, item * 2, 0)
    order[...] = one_hot(iota((ROWS, ROWS), 0) == target)

    key = iota((ROWS, 8 * TOK), 1)
    token = (key & (TOK - 1)) + row_index * TOK
    usable = ((key >> 4) == ((row >> 1) & 7)) & (token < lens)
    offset = (token - lens - step).astype(f32)
    tail_offset[...] = jnp.where(usable, offset, masked_score)

    row_prompt = row >> 5
    prompt_lens = jnp.where(
        row_prompt == 0, prefix_length[group * 2], prefix_length[group * 2 + 1]
    )
    query_pos = prompt_lens + own_lens + step
    lane = iota((1, GROUPS * TOK), 1)
    key_pos = (lane & (TOK - 1)) + row_index * TOK
    key_prompt = jnp.zeros((1, GROUPS * TOK), jnp.int32)
    for h in range(GROUPS):
        item = prefix_item[h * GROUPS + group]
        here = (lane >> 4) == h
        key_pos = key_pos + jnp.where(here, (item & (MAXPAGES - 1)) * PAGE, 0)
        key_prompt = jnp.where(here, (item >> 3) - group * 2, key_prompt)
    usable = (key_prompt == row_prompt) & (key_pos < prompt_lens)
    offset = (key_pos - query_pos).astype(f32)
    prefix_offset[...] = jnp.where(usable, offset, masked_score)

    table = small[...].astype(f32)

    def line(at):
        return jnp.concatenate([table[at : at + 1], table[at + 1 : at + 2]], axis=1)

    share = BLOCK // NCOL
    place = own_columns()

    def placed(values):
        return dot(jnp.broadcast_to(values, (8, share)).astype(bf16), place)[0:1]

    base[...] = dot(residual[...], place) + placed(table[13:14, 64:128])
    rows = [line(0), line(4), line(8), placed(table[14:15, 0:64]), line(10), line(12), line(2), line(6)]
    edge = iota((8, BLOCK), 0)
    filled = jnp.zeros((8, BLOCK), f32)
    for at, values in enumerate(rows):
        filled = jnp.where(edge == at, values, filled)
    vectors[...] = filled


def tail_kernel(recv, tails, distance, out, query, wide):
    first_head = lax.axis_index("col") * HEADS
    distance = distance[...]
    usable = distance > 0.5 * masked_score
    for g in range(GROUPS):
        rows = recv[g, KEYROWS:].astype(f32)
        for head in range(HEADS):
            query[head, 4 * g : 4 * g + 4] = rows[4 * head : 4 * head + 4]
    some = ROWS * 8 // TAILS
    blocks = ROWS // some
    stats = jnp.zeros((ROWS, 128), f32)
    scores, weights = [], []
    for head in range(HEADS):
        at = slice(head * HD, (head + 1) * HD)
        q = query[head].astype(bf16)
        parts = []
        for n in range(blocks):
            k = tails[8 * n : 8 * n + 8, 0, :, at].reshape(8 * TOK, HD)
            parts.append(dot_t(q[n * some : (n + 1) * some], k))
        scores.append(jnp.concatenate(parts, axis=0))
    for head in range(HEADS):
        biased = scores[head] * (1.0 / math.sqrt(HD)) + slope_of(first_head + head) * distance
        biased = jnp.where(usable, biased, masked_score)
        m = rounded(jnp.max(biased, axis=1, keepdims=True))
        shares = jnp.where(usable, jnp.exp(biased - m), 0.0)
        stats = put_stats(stats, head, m, jnp.sum(shares, axis=1, keepdims=True))
        weights.append(shares.astype(bf16))
    for head in range(HEADS):
        at = slice(head * HD, (head + 1) * HD)
        for n in range(blocks):
            v = tails[8 * n : 8 * n + 8, 1, :, at].reshape(8 * TOK, HD)
            rows = slice(n * some, (n + 1) * some)
            wide[rows, at] = dot(weights[head][rows], v)
    wide[:, WIDE:PACK] = stats
    for g in range(GROUPS):
        out[g] = wide[4 * g : 4 * g + 4].astype(bf16)


def prefix_kernel(
    fresh, recv, distance, vectors, up_weight, qkv_weight, out, up_rows, qkv_rows
):
    both = gain_rows(vectors[0:1], vectors[6:7])
    edge = iota((8, BLOCK), 0)
    for n in range(NROW):
        parts = dot(both, up_weight[:, n * BLOCK : (n + 1) * BLOCK])
        rows = jnp.zeros((8, BLOCK), f32)
        for at, values in enumerate(split(parts[0:1]) + split(parts[1:2])):
            rows = jnp.where(edge == at, values, rows)
        up_rows[n] = rows
    both = gain_rows(vectors[1:2], vectors[7:8])
    width = qkv_weight.shape[1] // NROW
    edge, blank = iota((8, 128), 0), jnp.zeros((8, 64), f32)
    for n in range(NROW):
        parts = dot(both, qkv_weight[:, n * width : (n + 1) * width])[0:8]
        rest = jnp.concatenate([blank, parts[:, 128:width]], axis=1)
        rows = jnp.where(edge < 2, parts[:, 0:128], 0.0)
        rows = jnp.where(edge == 2, rest[0:1], rows)
        qkv_rows[n] = jnp.where(edge == 3, rest[1:2], rows)

    distance = distance[...]
    usable = distance > 0.5 * masked_score
    row_index = lax.axis_index("row")
    first_head = lax.axis_index("col") * HEADS
    row = iota((ROWS, 1), 0)
    keys = GROUPS * TOK
    col = iota((ROWS, ROWS), 1)
    new_usable = ((col >> 1) == (row >> 1)) & ((col & 1) <= (row & 1)) & (row_index == 0)
    new_offset = ((col & 1) - (row & 1)).astype(f32)
    stats = jnp.zeros((ROWS, 128), f32)
    for head in range(HEADS):
        at = slice(head * HD, (head + 1) * HD)
        q = fresh[:, head * HD : (head + 1) * HD]
        new_k = fresh[:, WIDE + head * HD : WIDE + (head + 1) * HD]
        new_v = fresh[:, 2 * WIDE + head * HD : 2 * WIDE + (head + 1) * HD]
        k = recv[:, head * TOK : (head + 1) * TOK].reshape(keys, HD)
        v = recv[:, (HEADS + head) * TOK : (HEADS + head + 1) * TOK].reshape(keys, HD)
        slope = slope_of(first_head + head)
        scores = dot_t(q, k) * (1.0 / math.sqrt(HD)) + slope * distance
        scores = jnp.where(usable, scores, masked_score)
        new_scores = dot_t(q, new_k) * (1.0 / math.sqrt(HD)) + slope * new_offset
        new_scores = jnp.where(new_usable, new_scores, masked_score)
        m = rounded(
            jnp.maximum(
                jnp.max(scores, axis=1, keepdims=True),
                jnp.max(new_scores, axis=1, keepdims=True),
            )
        )
        weights = jnp.where(usable, jnp.exp(scores - m), 0.0)
        new_weights = jnp.where(new_usable, jnp.exp(new_scores - m), 0.0)
        total = jnp.sum(weights, axis=1, keepdims=True) + jnp.sum(
            new_weights, axis=1, keepdims=True
        )
        stats = put_stats(stats, head, m, total)
        out[:, at] = dot(weights.astype(bf16), v) + dot(new_weights.astype(bf16), new_v)
    out[:, WIDE:PACK] = stats


def columns_of(rows, other):
    return lax.dot_general(
        rows.astype(bf16), other.astype(bf16), (((0,), (0,)), ((), ())), preferred_element_type=f32
    )


def head_spread():
    return one_hot((iota((16, WIDE), 0) & 7) == (iota((16, WIDE), 1) >> 7))


def join_kernel(order, prefix, recv, out, wide):
    for h in range(GROUPS):
        wide[4 * h : 4 * h + 4] = recv[h].astype(f32)
    row, lane = iota((16, 128), 0), iota((16, 128), 1)
    head = (row & 7) * 4
    first = jnp.where(row < 8, head, head + 1)
    last = jnp.where(row < 8, head, head + 2)
    chosen = one_hot((lane >= first) & (lane <= last) & ((row & 7) < HEADS))
    left = dot_t(chosen, prefix[:, WIDE:PACK].astype(bf16))
    tails = dot(order[...], wide[...].astype(bf16))
    right = dot_t(chosen, tails[:, WIDE:PACK].astype(bf16))
    m = jnp.maximum(left[0:8], right[0:8])
    left_scale = jnp.exp(left[0:8] - m)
    right_scale = jnp.exp(right[0:8] - m)
    total = split(left_scale * left[8:16] + right_scale * right[8:16])
    spread = head_spread()
    left_scale = columns_of(jnp.concatenate(split(left_scale), axis=0), spread)
    right_scale = columns_of(jnp.concatenate(split(right_scale), axis=0), spread)
    joined = (left_scale * prefix[:, 0:WIDE] + right_scale * tails[:, 0:WIDE]).astype(bf16)
    blank = jnp.zeros((8, 128 - ROWS), f32)
    parts = []
    for part in (m,) + total:
        parts = parts + [part, blank]
    stats = jnp.concatenate(parts, axis=1).astype(bf16)
    for n in range(NROW):
        out[n, 0:ROWS] = joined
        out[n, ROWS : ROWS + 8, 0:384] = stats
        out[n, ROWS : ROWS + 8, 384:WIDE] = jnp.zeros((8, WIDE - 384), bf16)


def out_kernel(recv, weight, base, out):
    tables = [recv[n, ROWS : ROWS + 8, 0:384].astype(f32) for n in range(NROW)]
    maxima = [table[:, 0:ROWS] for table in tables]
    m = maxima[0]
    for part in maxima[1:]:
        m = jnp.maximum(m, part)
    scales = [jnp.exp(part - m) for part in maxima]
    sums = [table[:, 128 : 128 + ROWS] + table[:, 256 : 256 + ROWS] for table in tables]
    total = scales[0] * sums[0]
    for n in range(1, NROW):
        total = total + scales[n] * sums[n]
    spread = head_spread()
    inverse = jnp.where(iota((8, ROWS), 0) < HEADS, 1.0 / total, 0.0)
    attended = jnp.zeros((ROWS, WIDE), f32)
    for n in range(NROW):
        factor = jnp.concatenate(split(scales[n] * inverse), axis=0)
        attended = attended + columns_of(factor, spread) * recv[n, 0:ROWS].astype(f32)
    partial = (dot(attended.astype(bf16), weight[...]) + base[...]).astype(bf16)
    for n in range(NCOL):
        out[n] = partial


def centred(values, gain):
    mean = jnp.mean(values, axis=1, keepdims=True)
    away = values - mean
    return mean, jnp.sum(away * away, axis=1, keepdims=True), (away * gain).astype(bf16)


def as_rows(columns, order=None):
    lane = iota((ROWS, 8), 1)
    table = jnp.zeros((ROWS, 8), f32)
    for at, column in columns:
        table = jnp.where(lane == at, column, table)
    if order is None:
        order = iota((ROWS, ROWS), 1)
    order = one_hot(iota((ROWS, ROWS), 0) == order)
    return lax.dot_general(
        table.astype(bf16), order, (((0,), (0,)), ((), ())), preferred_element_type=f32
    )


def up_kernel(recv, vectors, extra, weight, hidden, out):
    values = recv[0].astype(f32)
    for n in range(1, NCOL):
        values = values + recv[n].astype(f32)
    hidden[...] = values
    mean, spread, scaled = centred(values, vectors[0:1])
    rows = as_rows(list(zip((4, 5, 6, 7), split(mean) + split(spread))))
    rows = jnp.concatenate([rows, jnp.zeros((8, BLOCK - ROWS), f32)], axis=1)
    edge = iota((8, BLOCK), 0)
    for n in range(NROW):
        out[n, 0:ROWS] = dot(scaled, weight[:, n * BLOCK : (n + 1) * BLOCK]).astype(bf16)
        out[n, ROWS : ROWS + 8] = jnp.where(edge < 4, extra[n], rows).astype(bf16)


def normed(total, bias, gains, shifts, means, spreads):
    width = total.shape[1]
    away = means - jnp.mean(means, axis=0, keepdims=True)
    spread = jnp.sum(spreads + BLOCK * away * away, axis=0, keepdims=True)
    scale = lax.rsqrt(spread / D + norm_eps)
    high, low = split(away)
    lefts = [high, low] * len(gains)
    rights = [part for part in gains for _ in range(2)]
    fixed = columns_of(jnp.concatenate(lefts, axis=0), jnp.concatenate(rights, axis=0))
    shifted = bias + sum(jnp.sum(part, axis=0, keepdims=True) for part in shifts)
    high, rest = split(scale)
    middle, low = split(rest)
    at = iota((8, ROWS), 0)
    parts = jnp.where(at == 0, high, jnp.where(at == 1, middle, jnp.where(at == 2, low, 0.0)))
    scales = columns_of(parts, jnp.ones((8, width), f32))
    return (total + fixed) * scales + shifted


def summed(recv, first, last):
    total = recv[0, first:last].astype(f32)
    for n in range(1, NROW):
        total = total + recv[n, first:last].astype(f32)
    return total


def hidden_kernel(recv, vectors, out, edges):
    for n in range(NROW):
        edge = recv[n, ROWS : ROWS + 8].astype(f32)
        edges[0, 8 * n : 8 * n + 8] = edge[:, 0:128]
        edges[1, 8 * n : 8 * n + 8] = edge[:, 128:BLOCK]

    def row(at):
        halves = [edges[half, pl.ds(at, NROW, stride=8), :] for half in range(2)]
        return jnp.concatenate(halves, axis=1)

    means = (row(4) + row(5))[:, 0:ROWS]
    spreads = (row(6) + row(7))[:, 0:ROWS]
    total = summed(recv, 0, ROWS)
    v = normed(total, vectors[4:5], [row(0), row(1)], [row(2), row(3)], means, spreads)
    v = 0.5 * v * (1.0 + jnp.tanh(math.sqrt(2.0 / math.pi) * (v + 0.044715 * (v * v * v))))
    v = v.astype(bf16)
    for n in range(NROW):
        out[n] = v


def down_kernel(recv, weight, vectors, out):
    total = vectors[3:4]
    for n in range(NROW):
        total = total + dot(recv[n], weight[n * BLOCK : (n + 1) * BLOCK])
    total = total.astype(bf16)
    for n in range(NCOL):
        out[n] = total


def next_kernel(recv, hidden, vectors, extra, weight, layer_out, out):
    values = hidden[...]
    for n in range(NCOL):
        values = values + recv[n].astype(f32)
    low = values.astype(bf16)
    values = low.astype(f32)
    layer_out[...] = dot_t(low, own_columns()).astype(bf16)
    mean, spread, scaled = centred(values, vectors[1:2])
    scores = jnp.sum(values * vectors[2:3], axis=1, keepdims=True)
    lane = iota((ROWS, ROWS), 1)
    by_step = ((lane & 31) << 1) + (lane >> 5)
    rows = as_rows(list(zip((2, 3, 4, 5), split(mean) + split(spread))))
    rows = rows + as_rows(list(zip((6, 7), split(scores))), by_step)
    width = weight.shape[1] // NROW
    half = ROWS // 2
    rows = jnp.concatenate([rows, jnp.zeros((8, 128 - ROWS), f32)], axis=1)
    for n in range(NROW):
        part = dot(scaled, weight[:, n * width : (n + 1) * width])
        rest = part[:, 128:width]
        rest = jnp.concatenate([rest[0:half], rest[half:ROWS]], axis=1)
        out[n, 0:ROWS] = part[:, 0:128].astype(bf16)
        out[n, ROWS : ROWS + half] = rest.astype(bf16)
        out[n, ROWS + half : ROWS + half + 8] = (extra[n] + rows).astype(bf16)


def final_kernel(recv, vectors, projected_next, score_out, wide, edges):
    width = projected_next.shape[2]
    half = ROWS // 2
    for n in range(NROW):
        edges[8 * n : 8 * n + 8] = recv[n, ROWS + half : ROWS + half + 8].astype(f32)

    def row(at):
        return edges[pl.ds(at, NROW, stride=8), :]

    second, third = row(2), row(3)
    gain = jnp.concatenate([row(0), second[:, 64:128]], axis=1)
    shift = jnp.concatenate([row(1), third[:, 64:128]], axis=1)
    means = (second + third)[:, 0:ROWS]
    spreads = (row(4) + row(5))[:, 0:ROWS]
    rest = summed(recv, ROWS, ROWS + half)
    rest = jnp.concatenate([rest[:, 0:64], rest[:, 64:128]], axis=0)
    total = jnp.concatenate([summed(recv, 0, ROWS), rest], axis=1)
    wide[...] = normed(total, vectors[5:6, 0:width], [gain], [shift], means, spreads)
    for i in range(ROWS // 2):
        projected_next[i] = wide[2 * i : 2 * i + 2].astype(bf16)
    total = jnp.sum(row(6) + row(7), axis=0, keepdims=True)
    score_out[0:1] = total[:, 0:half]
    score_out[1:2] = total[:, half:ROWS]


def call(kernel, out, scalars, arrays, scratch=(), remote=(), limit=16, home=pltpu.VMEM):
    many = isinstance(out, list)
    outs = out if many else [out]
    moved = sum(a.size * a.dtype.itemsize for a in arrays)
    moved += sum(math.prod(s) * jnp.dtype(t).itemsize for s, t in outs)
    shapes = [jax.ShapeDtypeStruct(s, t) for s, t in outs]
    vmem = pl.BlockSpec(memory_space=pltpu.VMEM)
    specs = [pl.BlockSpec(memory_space=pltpu.HBM)] * len(remote)
    specs += [pl.BlockSpec(memory_space=pltpu.SMEM)] * len(scalars) + [vmem] * len(arrays)
    return pl.pallas_call(
        kernel,
        out_shape=shapes if many else shapes[0],
        in_specs=specs,
        out_specs=[vmem] * len(outs) if many else pl.BlockSpec(memory_space=home),
        scratch_shapes=scratch,
        cost_estimate=pl.CostEstimate(flops=0, bytes_accessed=moved, transcendentals=0),
        compiler_params=pltpu.CompilerParams(vmem_limit_bytes=limit * 1024 * 1024),
        name=kernel.__name__,
    )(*remote, *scalars, *arrays)


def exchange(x, axis):
    return lax.all_to_all(x, axis, split_axis=0, concat_axis=0, tiled=True)


def shards(
    residual,
    fresh_qkv,
    prefix_pages,
    tail_pages,
    prefix_item,
    tail_item,
    prefix_length,
    tail_length,
    out_weight,
    out_bias,
    mlp_gain,
    mlp_shift,
    up_weight,
    up_bias,
    down_weight,
    down_bias,
    next_gain,
    next_shift,
    score_weight,
    qkv_weight,
    qkv_bias,
):
    cont_local = residual.shape[0]
    share = residual.shape[2]
    width = qkv_bias.shape[0]

    small = jnp.concatenate(
        [
            mlp_gain,
            mlp_shift,
            next_gain,
            next_shift,
            score_weight,
            up_bias,
            qkv_bias,
            out_bias,
            down_bias,
            jnp.zeros((192,), bf16),
        ]
    ).reshape(16, 128)
    stored = jnp.swapaxes(fresh_qkv, 1, 2).reshape(cont_local, 3, 2, WIDE)
    sent = call(
        send_kernel,
        ((GROUPS, KEYROWS + TOK, HD), bf16),
        [],
        [],
        [
            pltpu.VMEM((4, 128), jnp.int32),
            pltpu.VMEM((cont_local, 2, WIDE), bf16),
            pltpu.VMEM((ROWS, WIDE), f32),
            pltpu.VMEM((GROUPS * TOK, HD), f32),
            pltpu.VMEM((GROUPS, KEYROWS + TOK, HD), bf16),
            pltpu.SemaphoreType.DMA((2 + 2 * HEADS,)),
            pltpu.SemaphoreType.DMA((1 + 2 * HEADS,)),
        ],
        [tail_item.reshape(4, 128), stored, prefix_pages],
        60,
        pltpu.HBM,
    )
    arrived = exchange(sent, "pages")
    tail_offset, prefix_offset, order, base, vectors = call(
        ready_kernel,
        [
            ((ROWS, 8 * TOK), f32),
            ((ROWS, GROUPS * TOK), f32),
            ((ROWS, ROWS), bf16),
            ((ROWS, BLOCK), f32),
            ((8, BLOCK), f32),
        ],
        [tail_item, tail_length, prefix_item, prefix_length],
        [residual.reshape(ROWS, share), small],
    )
    tails = call(
        tail_kernel,
        ((GROUPS, 4, PACK), bf16),
        [],
        [arrived, tail_pages, tail_offset],
        [pltpu.VMEM((HEADS, ROWS, HD), f32), pltpu.VMEM((ROWS, PACK), f32)],
    )
    tails = exchange(tails, "pages")
    prefix, up_rows, qkv_rows = call(
        prefix_kernel,
        [((ROWS, PACK), f32), ((NROW, 8, BLOCK), f32), ((NROW, 8, 128), f32)],
        [],
        [
            fresh_qkv.reshape(ROWS, 3 * WIDE),
            arrived,
            prefix_offset,
            vectors,
            up_weight,
            qkv_weight,
        ],
    )
    joined = call(
        join_kernel,
        ((NROW, ROWS + 8, WIDE), bf16),
        [],
        [order, prefix, tails],
        [pltpu.VMEM((ROWS, PACK), f32)],
    )
    joined = exchange(joined, "row")
    partial = call(
        out_kernel,
        ((NCOL, ROWS, BLOCK), bf16),
        [],
        [joined, out_weight, base],
    )
    partial = exchange(partial, "col")
    hidden_one, partial = call(
        up_kernel,
        [((ROWS, BLOCK), f32), ((NROW, ROWS + 8, BLOCK), bf16)],
        [],
        [partial, vectors, up_rows, up_weight],
    )
    partial = exchange(partial, "row")
    hidden_two = call(
        hidden_kernel,
        ((NROW, ROWS, BLOCK), bf16),
        [],
        [partial, vectors],
        [pltpu.VMEM((2, ROWS, 128), f32)],
    )
    hidden_two = exchange(hidden_two, "row")
    partial = call(
        down_kernel, ((NCOL, ROWS, BLOCK), bf16), [], [hidden_two, down_weight, vectors]
    )
    partial = exchange(partial, "col")
    layer_out, partial = call(
        next_kernel,
        [((ROWS, share), bf16), ((NROW, ROWS + ROWS // 2 + 8, 128), bf16)],
        [],
        [partial, hidden_one, vectors, qkv_rows, qkv_weight],
    )
    partial = exchange(partial, "row")
    projected_next, score_sum = call(
        final_kernel,
        [((cont_local, 2, width), bf16), ((2, cont_local), f32)],
        [],
        [partial, vectors],
        [pltpu.VMEM((ROWS, width), f32), pltpu.VMEM((ROWS, 128), f32)],
    )
    return (layer_out.reshape(cont_local, 2, share), score_sum.T, projected_next)


def solution(mesh):
    in_specs = (
        P("pages", None, ("row", "col")),
        P("pages", None, None, "col"),
        P("pages", None, "row", "col"),
        P("pages", None, "row", "col"),
        P(),
        P(),
        P(),
        P(),
        P("col", "row"),
        P(("row", "col")),
        P("row"),
        P("row"),
        P("row", "col"),
        P(("col", "row")),
        P("col", "row"),
        P(("row", "col")),
        P("row"),
        P("row"),
        P("row"),
        P("row", "col"),
        P(("col", "row")),
    )
    out_specs = (
        P("pages", None, ("row", "col")),
        P("pages", None),
        P("pages", None, ("col", "row")),
    )
    return jax.shard_map(shards, mesh=mesh, in_specs=in_specs, out_specs=out_specs, check_vma=False)
```

```python
import math

import jax
import jax.numpy as jnp
from jax import lax
from jax.experimental import pallas as pl
from jax.experimental.pallas import tpu as pltpu
from jax.sharding import PartitionSpec as P

D = 2048
H = 16
HD = 128
PAGE = 128
MAXPAGES = 8
CONT = 16

GROUPS = 16
NROW = 8
NCOL = 4
ROWS = 64
HEADS = 4
WIDE = HEADS * HD
PACK = WIDE + 128
BLOCK = D // NROW
TOK = 16
TAILS = 32
KEYROWS = 2 * HEADS * TOK

masked_score = -1e30
norm_eps = 1e-05
f32 = jnp.float32
bf16 = jnp.bfloat16


def dot(a, b):
    return jnp.dot(a, b, preferred_element_type=f32)


def dot_t(a, b):
    return lax.dot_general(a, b, (((1,), (1,)), ((), ())), preferred_element_type=f32)


def iota(shape, dim):
    return lax.broadcasted_iota(jnp.int32, shape, dim)


def one_hot(mask):
    return jnp.where(mask, 1.0, 0.0).astype(bf16)


def rounded(x):
    return x.astype(bf16).astype(f32)


def slope_of(head):
    return jnp.exp2(jnp.full((ROWS, 1), -8.0 / H, f32) * (head + 1).astype(f32))


def put_stats(stats, head, m, l):
    lane = iota((ROWS, 128), 1)
    hi = rounded(l)
    stats = jnp.where(lane == head * 4, m, stats)
    stats = jnp.where(lane == head * 4 + 1, hi, stats)
    return jnp.where(lane == head * 4 + 2, l - hi, stats)


def send_kernel(tail_item, fresh, pages, out, items, query, wide, rows, stage, sems, out_sems):
    copies = [
        pltpu.make_async_copy(tail_item, items, sems.at[0]),
        pltpu.make_async_copy(fresh.at[:, 0], query, sems.at[1]),
    ]
    for n in range(2 * HEADS):
        head = slice((n % HEADS) * HD, (n % HEADS + 1) * HD)
        copies.append(
            pltpu.make_async_copy(
                pages.at[:, n // HEADS, :, head],
                stage.at[:, n * TOK : (n + 1) * TOK],
                sems.at[2 + n],
            )
        )
    for copy in copies:
        copy.start()
    group = lax.axis_index("pages")
    source, lane = iota((128, ROWS), 0), iota((128, ROWS), 1)
    place = (((lane >> 2) & 3) == (source >> 5)) & (
        (source & (TAILS - 1)) == group * 2 + ((lane >> 1) & 1)
    )
    place = one_hot(place)
    copies[0].wait()
    local = (items[...] & (TAILS - 1)).astype(f32).astype(bf16)
    found = dot(local, place)
    here = iota(found.shape, 0) == (iota(found.shape, 1) >> 4)
    target = jnp.sum(jnp.where(here, found, 0.0), axis=0, keepdims=True).astype(jnp.int32) * 2
    target = target + (iota((1, ROWS), 1) & 1)
    pick = one_hot(iota((ROWS, ROWS), 0) == target)
    copies[1].wait()
    for j in range(TAILS):
        wide[2 * j : 2 * j + 2] = query[j].astype(f32)
    leaving = []
    for n in range(2 * HEADS):
        part = slice(n * TOK, (n + 1) * TOK)
        copies[2 + n].wait()
        leaving.append(pltpu.make_async_copy(stage.at[:, part], out.at[:, part], out_sems.at[n]))
        leaving[n].start()
    picked = lax.dot_general(
        pick, wide[...].astype(bf16), (((0,), (0,)), ((), ())), preferred_element_type=f32
    )
    for h in range(GROUPS):
        for head in range(HEADS):
            at = h * TOK + head * 4
            rows[at : at + 4] = picked[4 * h : 4 * h + 4, head * HD : (head + 1) * HD]
    stage[:, KEYROWS:] = rows[...].reshape(GROUPS, TOK, HD).astype(bf16)
    last = pltpu.make_async_copy(
        stage.at[:, KEYROWS : KEYROWS + TOK],
        out.at[:, KEYROWS : KEYROWS + TOK],
        out_sems.at[2 * HEADS],
    )
    last.start()
    for copy in leaving + [last]:
        copy.wait()


def own_columns():
    share = BLOCK // NCOL
    first = lax.axis_index("col") * share
    return one_hot(iota((share, BLOCK), 1) == iota((share, BLOCK), 0) + first)


def gain_rows(gain, shift):
    row = iota((16, BLOCK), 0)
    return jnp.where(row == 0, gain, jnp.where(row == 1, shift, 0.0)).astype(bf16)


def split(x):
    hi = rounded(x)
    return hi, x - hi


def ready_kernel(
    tail_item,
    tail_length,
    prefix_item,
    prefix_length,
    residual,
    small,
    tail_offset,
    prefix_offset,
    order,
    base,
    vectors,
):
    group = lax.axis_index("pages")
    row_index = lax.axis_index("row")
    row = iota((ROWS, 1), 0)
    step = row & 1
    lens = jnp.zeros((ROWS, 1), jnp.int32)
    own_lens = jnp.zeros((ROWS, 1), jnp.int32)
    lane = iota((1, ROWS), 1)
    target = lane & 1
    for j in range(TAILS):
        here = (row >> 1) == j
        lens = jnp.where(here, tail_length[tail_item[group * TAILS + j]], lens)
        own_lens = jnp.where(here, tail_length[group * TAILS + j], own_lens)
        item = tail_item[(j // 2) * TAILS + group * 2 + j % 2] - group * TAILS
        target = target + jnp.where((lane >> 1) == j, item * 2, 0)
    order[...] = one_hot(iota((ROWS, ROWS), 0) == target)

    key = iota((ROWS, 8 * TOK), 1)
    token = (key & (TOK - 1)) + row_index * TOK
    usable = ((key >> 4) == ((row >> 1) & 7)) & (token < lens)
    offset = (token - lens - step).astype(f32)
    tail_offset[...] = jnp.where(usable, offset, masked_score)

    row_prompt = row >> 5
    prompt_lens = jnp.where(
        row_prompt == 0, prefix_length[group * 2], prefix_length[group * 2 + 1]
    )
    query_pos = prompt_lens + own_lens + step
    lane = iota((1, GROUPS * TOK), 1)
    key_pos = (lane & (TOK - 1)) + row_index * TOK
    key_prompt = jnp.zeros((1, GROUPS * TOK), jnp.int32)
    for h in range(GROUPS):
        item = prefix_item[h * GROUPS + group]
        here = (lane >> 4) == h
        key_pos = key_pos + jnp.where(here, (item & (MAXPAGES - 1)) * PAGE, 0)
        key_prompt = jnp.where(here, (item >> 3) - group * 2, key_prompt)
    usable = (key_prompt == row_prompt) & (key_pos < prompt_lens)
    offset = (key_pos - query_pos).astype(f32)
    prefix_offset[...] = jnp.where(usable, offset, masked_score)

    table = small[...].astype(f32)

    def line(at):
        return jnp.concatenate([table[at : at + 1], table[at + 1 : at + 2]], axis=1)

    share = BLOCK // NCOL
    place = own_columns()

    def placed(values):
        return dot(jnp.broadcast_to(values, (8, share)).astype(bf16), place)[0:1]

    base[...] = dot(residual[...], place) + placed(table[13:14, 64:128])
    rows = [line(0), line(4), line(8), placed(table[14:15, 0:64]), line(10), line(12), line(2), line(6)]
    edge = iota((8, BLOCK), 0)
    filled = jnp.zeros((8, BLOCK), f32)
    for at, values in enumerate(rows):
        filled = jnp.where(edge == at, values, filled)
    vectors[...] = filled


def tail_kernel(recv, tails, distance, out, query, wide):
    first_head = lax.axis_index("col") * HEADS
    distance = distance[...]
    usable = distance > 0.5 * masked_score
    for g in range(GROUPS):
        rows = recv[g, KEYROWS:].astype(f32)
        for head in range(HEADS):
            query[head, 4 * g : 4 * g + 4] = rows[4 * head : 4 * head + 4]
    some = ROWS * 8 // TAILS
    blocks = ROWS // some
    stats = jnp.zeros((ROWS, 128), f32)
    scores, weights = [], []
    for head in range(HEADS):
        at = slice(head * HD, (head + 1) * HD)
        q = query[head].astype(bf16)
        parts = []
        for n in range(blocks):
            k = tails[8 * n : 8 * n + 8, 0, :, at].reshape(8 * TOK, HD)
            parts.append(dot_t(q[n * some : (n + 1) * some], k))
        scores.append(jnp.concatenate(parts, axis=0))
    for head in range(HEADS):
        biased = scores[head] * (1.0 / math.sqrt(HD)) + slope_of(first_head + head) * distance
        biased = jnp.where(usable, biased, masked_score)
        m = rounded(jnp.max(biased, axis=1, keepdims=True))
        shares = jnp.where(usable, jnp.exp(biased - m), 0.0)
        stats = put_stats(stats, head, m, jnp.sum(shares, axis=1, keepdims=True))
        weights.append(shares.astype(bf16))
    for head in range(HEADS):
        at = slice(head * HD, (head + 1) * HD)
        for n in range(blocks):
            v = tails[8 * n : 8 * n + 8, 1, :, at].reshape(8 * TOK, HD)
            rows = slice(n * some, (n + 1) * some)
            wide[rows, at] = dot(weights[head][rows], v)
    wide[:, WIDE:PACK] = stats
    for g in range(GROUPS):
        out[g] = wide[4 * g : 4 * g + 4].astype(bf16)


def prefix_kernel(
    fresh, recv, distance, vectors, up_weight, qkv_weight, out, up_rows, qkv_rows
):
    both = gain_rows(vectors[0:1], vectors[6:7])
    edge = iota((8, BLOCK), 0)
    for n in range(NROW):
        parts = dot(both, up_weight[:, n * BLOCK : (n + 1) * BLOCK])
        rows = jnp.zeros((8, BLOCK), f32)
        for at, values in enumerate(split(parts[0:1]) + split(parts[1:2])):
            rows = jnp.where(edge == at, values, rows)
        up_rows[n] = rows
    both = gain_rows(vectors[1:2], vectors[7:8])
    width = qkv_weight.shape[1] // NROW
    edge, blank = iota((8, 128), 0), jnp.zeros((8, 64), f32)
    for n in range(NROW):
        parts = dot(both, qkv_weight[:, n * width : (n + 1) * width])[0:8]
        rest = jnp.concatenate([blank, parts[:, 128:width]], axis=1)
        rows = jnp.where(edge < 2, parts[:, 0:128], 0.0)
        rows = jnp.where(edge == 2, rest[0:1], rows)
        qkv_rows[n] = jnp.where(edge == 3, rest[1:2], rows)

    distance = distance[...]
    usable = distance > 0.5 * masked_score
    row_index = lax.axis_index("row")
    first_head = lax.axis_index("col") * HEADS
    row = iota((ROWS, 1), 0)
    keys = GROUPS * TOK
    col = iota((ROWS, ROWS), 1)
    new_usable = ((col >> 1) == (row >> 1)) & ((col & 1) <= (row & 1)) & (row_index == 0)
    new_offset = ((col & 1) - (row & 1)).astype(f32)
    stats = jnp.zeros((ROWS, 128), f32)
    for head in range(HEADS):
        at = slice(head * HD, (head + 1) * HD)
        q = fresh[:, head * HD : (head + 1) * HD]
        new_k = fresh[:, WIDE + head * HD : WIDE + (head + 1) * HD]
        new_v = fresh[:, 2 * WIDE + head * HD : 2 * WIDE + (head + 1) * HD]
        k = recv[:, head * TOK : (head + 1) * TOK].reshape(keys, HD)
        v = recv[:, (HEADS + head) * TOK : (HEADS + head + 1) * TOK].reshape(keys, HD)
        slope = slope_of(first_head + head)
        scores = dot_t(q, k) * (1.0 / math.sqrt(HD)) + slope * distance
        scores = jnp.where(usable, scores, masked_score)
        new_scores = dot_t(q, new_k) * (1.0 / math.sqrt(HD)) + slope * new_offset
        new_scores = jnp.where(new_usable, new_scores, masked_score)
        m = rounded(
            jnp.maximum(
                jnp.max(scores, axis=1, keepdims=True),
                jnp.max(new_scores, axis=1, keepdims=True),
            )
        )
        weights = jnp.where(usable, jnp.exp(scores - m), 0.0)
        new_weights = jnp.where(new_usable, jnp.exp(new_scores - m), 0.0)
        total = jnp.sum(weights, axis=1, keepdims=True) + jnp.sum(
            new_weights, axis=1, keepdims=True
        )
        stats = put_stats(stats, head, m, total)
        out[:, at] = dot(weights.astype(bf16), v) + dot(new_weights.astype(bf16), new_v)
    out[:, WIDE:PACK] = stats


def columns_of(rows, other):
    return lax.dot_general(
        rows.astype(bf16), other.astype(bf16), (((0,), (0,)), ((), ())), preferred_element_type=f32
    )


def head_spread():
    return one_hot((iota((16, WIDE), 0) & 7) == (iota((16, WIDE), 1) >> 7))


def join_kernel(order, prefix, recv, out, wide):
    for h in range(GROUPS):
        wide[4 * h : 4 * h + 4] = recv[h].astype(f32)
    row, lane = iota((16, 128), 0), iota((16, 128), 1)
    head = (row & 7) * 4
    first = jnp.where(row < 8, head, head + 1)
    last = jnp.where(row < 8, head, head + 2)
    chosen = one_hot((lane >= first) & (lane <= last) & ((row & 7) < HEADS))
    left = dot_t(chosen, prefix[:, WIDE:PACK].astype(bf16))
    tails = dot(order[...], wide[...].astype(bf16))
    right = dot_t(chosen, tails[:, WIDE:PACK].astype(bf16))
    m = jnp.maximum(left[0:8], right[0:8])
    left_scale = jnp.exp(left[0:8] - m)
    right_scale = jnp.exp(right[0:8] - m)
    total = split(left_scale * left[8:16] + right_scale * right[8:16])
    spread = head_spread()
    left_scale = columns_of(jnp.concatenate(split(left_scale), axis=0), spread)
    right_scale = columns_of(jnp.concatenate(split(right_scale), axis=0), spread)
    joined = (left_scale * prefix[:, 0:WIDE] + right_scale * tails[:, 0:WIDE]).astype(bf16)
    blank = jnp.zeros((8, 128 - ROWS), f32)
    parts = []
    for part in (m,) + total:
        parts = parts + [part, blank]
    stats = jnp.concatenate(parts, axis=1).astype(bf16)
    for n in range(NROW):
        out[n, 0:ROWS] = joined
        out[n, ROWS : ROWS + 8, 0:384] = stats
        out[n, ROWS : ROWS + 8, 384:WIDE] = jnp.zeros((8, WIDE - 384), bf16)


def out_kernel(recv, weight, base, out):
    tables = [recv[n, ROWS : ROWS + 8, 0:384].astype(f32) for n in range(NROW)]
    maxima = [table[:, 0:ROWS] for table in tables]
    m = maxima[0]
    for part in maxima[1:]:
        m = jnp.maximum(m, part)
    scales = [jnp.exp(part - m) for part in maxima]
    sums = [table[:, 128 : 128 + ROWS] + table[:, 256 : 256 + ROWS] for table in tables]
    total = scales[0] * sums[0]
    for n in range(1, NROW):
        total = total + scales[n] * sums[n]
    spread = head_spread()
    inverse = jnp.where(iota((8, ROWS), 0) < HEADS, 1.0 / total, 0.0)
    attended = jnp.zeros((ROWS, WIDE), f32)
    for n in range(NROW):
        factor = jnp.concatenate(split(scales[n] * inverse), axis=0)
        attended = attended + columns_of(factor, spread) * recv[n, 0:ROWS].astype(f32)
    partial = (dot(attended.astype(bf16), weight[...]) + base[...]).astype(bf16)
    for n in range(NCOL):
        out[n] = partial


def centred(values, gain):
    mean = jnp.mean(values, axis=1, keepdims=True)
    away = values - mean
    return mean, jnp.sum(away * away, axis=1, keepdims=True), (away * gain).astype(bf16)


def as_rows(columns, order=None):
    lane = iota((ROWS, 8), 1)
    table = jnp.zeros((ROWS, 8), f32)
    for at, column in columns:
        table = jnp.where(lane == at, column, table)
    if order is None:
        order = iota((ROWS, ROWS), 1)
    order = one_hot(iota((ROWS, ROWS), 0) == order)
    return lax.dot_general(
        table.astype(bf16), order, (((0,), (0,)), ((), ())), preferred_element_type=f32
    )


def up_kernel(recv, vectors, extra, weight, hidden, out):
    values = recv[0].astype(f32)
    for n in range(1, NCOL):
        values = values + recv[n].astype(f32)
    hidden[...] = values
    mean, spread, scaled = centred(values, vectors[0:1])
    rows = as_rows(list(zip((4, 5, 6, 7), split(mean) + split(spread))))
    rows = jnp.concatenate([rows, jnp.zeros((8, BLOCK - ROWS), f32)], axis=1)
    edge = iota((8, BLOCK), 0)
    for n in range(NROW):
        out[n, 0:ROWS] = dot(scaled, weight[:, n * BLOCK : (n + 1) * BLOCK]).astype(bf16)
        out[n, ROWS : ROWS + 8] = jnp.where(edge < 4, extra[n], rows).astype(bf16)


def normed(total, bias, gains, shifts, means, spreads):
    width = total.shape[1]
    away = means - jnp.mean(means, axis=0, keepdims=True)
    spread = jnp.sum(spreads + BLOCK * away * away, axis=0, keepdims=True)
    scale = lax.rsqrt(spread / D + norm_eps)
    high, low = split(away)
    lefts = [high, low] * len(gains)
    rights = [part for part in gains for _ in range(2)]
    fixed = columns_of(jnp.concatenate(lefts, axis=0), jnp.concatenate(rights, axis=0))
    shifted = bias + sum(jnp.sum(part, axis=0, keepdims=True) for part in shifts)
    high, rest = split(scale)
    middle, low = split(rest)
    at = iota((8, ROWS), 0)
    parts = jnp.where(at == 0, high, jnp.where(at == 1, middle, jnp.where(at == 2, low, 0.0)))
    scales = columns_of(parts, jnp.ones((8, width), f32))
    return (total + fixed) * scales + shifted


def summed(recv, first, last):
    total = recv[0, first:last].astype(f32)
    for n in range(1, NROW):
        total = total + recv[n, first:last].astype(f32)
    return total


def hidden_kernel(recv, vectors, out, edges):
    for n in range(NROW):
        edge = recv[n, ROWS : ROWS + 8].astype(f32)
        edges[0, 8 * n : 8 * n + 8] = edge[:, 0:128]
        edges[1, 8 * n : 8 * n + 8] = edge[:, 128:BLOCK]

    def row(at):
        halves = [edges[half, pl.ds(at, NROW, stride=8), :] for half in range(2)]
        return jnp.concatenate(halves, axis=1)

    means = (row(4) + row(5))[:, 0:ROWS]
    spreads = (row(6) + row(7))[:, 0:ROWS]
    total = summed(recv, 0, ROWS)
    v = normed(total, vectors[4:5], [row(0), row(1)], [row(2), row(3)], means, spreads)
    v = 0.5 * v * (1.0 + jnp.tanh(math.sqrt(2.0 / math.pi) * (v + 0.044715 * (v * v * v))))
    v = v.astype(bf16)
    for n in range(NROW):
        out[n] = v


def down_kernel(recv, weight, vectors, out):
    total = vectors[3:4]
    for n in range(NROW):
        total = total + dot(recv[n], weight[n * BLOCK : (n + 1) * BLOCK])
    total = total.astype(bf16)
    for n in range(NCOL):
        out[n] = total


def next_kernel(recv, hidden, vectors, extra, weight, own, out):
    values = hidden[...]
    for n in range(NCOL):
        values = values + recv[n].astype(f32)
    low = values.astype(bf16)
    values = low.astype(f32)
    own[...] = dot_t(low, own_columns()).astype(bf16)
    mean, spread, scaled = centred(values, vectors[1:2])
    scores = jnp.sum(values * vectors[2:3], axis=1, keepdims=True)
    lane = iota((ROWS, ROWS), 1)
    by_step = ((lane & 31) << 1) + (lane >> 5)
    rows = as_rows(list(zip((2, 3, 4, 5), split(mean) + split(spread))))
    rows = rows + as_rows(list(zip((6, 7), split(scores))), by_step)
    width = weight.shape[1] // NROW
    half = ROWS // 2
    rows = jnp.concatenate([rows, jnp.zeros((8, 128 - ROWS), f32)], axis=1)
    for n in range(NROW):
        part = dot(scaled, weight[:, n * width : (n + 1) * width])
        rest = part[:, 128:width]
        rest = jnp.concatenate([rest[0:half], rest[half:ROWS]], axis=1)
        out[n, 0:ROWS] = part[:, 0:128].astype(bf16)
        out[n, ROWS : ROWS + half] = rest.astype(bf16)
        out[n, ROWS + half : ROWS + half + 8] = (extra[n] + rows).astype(bf16)


def final_kernel(recv, vectors, own, layer_out, projected_next, score_out, wide, edges):
    layer_out[...] = own[...]
    width = projected_next.shape[2]
    half = ROWS // 2
    for n in range(NROW):
        edges[8 * n : 8 * n + 8] = recv[n, ROWS + half : ROWS + half + 8].astype(f32)

    def row(at):
        return edges[pl.ds(at, NROW, stride=8), :]

    second, third = row(2), row(3)
    gain = jnp.concatenate([row(0), second[:, 64:128]], axis=1)
    shift = jnp.concatenate([row(1), third[:, 64:128]], axis=1)
    means = (second + third)[:, 0:ROWS]
    spreads = (row(4) + row(5))[:, 0:ROWS]
    rest = summed(recv, ROWS, ROWS + half)
    rest = jnp.concatenate([rest[:, 0:64], rest[:, 64:128]], axis=0)
    total = jnp.concatenate([summed(recv, 0, ROWS), rest], axis=1)
    wide[...] = normed(total, vectors[5:6, 0:width], [gain], [shift], means, spreads)
    for i in range(ROWS // 2):
        projected_next[i] = wide[2 * i : 2 * i + 2].astype(bf16)
    total = jnp.sum(row(6) + row(7), axis=0, keepdims=True)
    score_out[0:1] = total[:, 0:half]
    score_out[1:2] = total[:, half:ROWS]


def call(kernel, out, scalars, arrays, scratch=(), remote=(), limit=16, home=pltpu.VMEM):
    many = isinstance(out, list)
    outs = out if many else [out]
    moved = sum(a.size * a.dtype.itemsize for a in arrays)
    moved += sum(math.prod(s) * jnp.dtype(t).itemsize for s, t in outs)
    shapes = [jax.ShapeDtypeStruct(s, t) for s, t in outs]
    vmem = pl.BlockSpec(memory_space=pltpu.VMEM)
    specs = [pl.BlockSpec(memory_space=pltpu.HBM)] * len(remote)
    specs += [pl.BlockSpec(memory_space=pltpu.SMEM)] * len(scalars) + [vmem] * len(arrays)
    return pl.pallas_call(
        kernel,
        out_shape=shapes if many else shapes[0],
        in_specs=specs,
        out_specs=[vmem] * len(outs) if many else pl.BlockSpec(memory_space=home),
        scratch_shapes=scratch,
        cost_estimate=pl.CostEstimate(flops=0, bytes_accessed=moved, transcendentals=0),
        compiler_params=pltpu.CompilerParams(vmem_limit_bytes=limit * 1024 * 1024),
        name=kernel.__name__,
    )(*remote, *scalars, *arrays)


def exchange(x, axis):
    return lax.all_to_all(x, axis, split_axis=0, concat_axis=0, tiled=True)


def shards(
    residual,
    fresh_qkv,
    prefix_pages,
    tail_pages,
    prefix_item,
    tail_item,
    prefix_length,
    tail_length,
    out_weight,
    out_bias,
    mlp_gain,
    mlp_shift,
    up_weight,
    up_bias,
    down_weight,
    down_bias,
    next_gain,
    next_shift,
    score_weight,
    qkv_weight,
    qkv_bias,
):
    cont_local = residual.shape[0]
    share = residual.shape[2]
    width = qkv_bias.shape[0]

    small = jnp.concatenate(
        [
            mlp_gain,
            mlp_shift,
            next_gain,
            next_shift,
            score_weight,
            up_bias,
            qkv_bias,
            out_bias,
            down_bias,
            jnp.zeros((192,), bf16),
        ]
    ).reshape(16, 128)
    stored = jnp.swapaxes(fresh_qkv, 1, 2).reshape(cont_local, 3, 2, WIDE)
    sent = call(
        send_kernel,
        ((GROUPS, KEYROWS + TOK, HD), bf16),
        [],
        [],
        [
            pltpu.VMEM((4, 128), jnp.int32),
            pltpu.VMEM((cont_local, 2, WIDE), bf16),
            pltpu.VMEM((ROWS, WIDE), f32),
            pltpu.VMEM((GROUPS * TOK, HD), f32),
            pltpu.VMEM((GROUPS, KEYROWS + TOK, HD), bf16),
            pltpu.SemaphoreType.DMA((2 + 2 * HEADS,)),
            pltpu.SemaphoreType.DMA((1 + 2 * HEADS,)),
        ],
        [tail_item.reshape(4, 128), stored, prefix_pages],
        60,
        pltpu.HBM,
    )
    arrived = exchange(sent, "pages")
    tail_offset, prefix_offset, order, base, vectors = call(
        ready_kernel,
        [
            ((ROWS, 8 * TOK), f32),
            ((ROWS, GROUPS * TOK), f32),
            ((ROWS, ROWS), bf16),
            ((ROWS, BLOCK), f32),
            ((8, BLOCK), f32),
        ],
        [tail_item, tail_length, prefix_item, prefix_length],
        [residual.reshape(ROWS, share), small],
    )
    tails = call(
        tail_kernel,
        ((GROUPS, 4, PACK), bf16),
        [],
        [arrived, tail_pages, tail_offset],
        [pltpu.VMEM((HEADS, ROWS, HD), f32), pltpu.VMEM((ROWS, PACK), f32)],
    )
    tails = exchange(tails, "pages")
    prefix, up_rows, qkv_rows = call(
        prefix_kernel,
        [((ROWS, PACK), f32), ((NROW, 8, BLOCK), f32), ((NROW, 8, 128), f32)],
        [],
        [
            fresh_qkv.reshape(ROWS, 3 * WIDE),
            arrived,
            prefix_offset,
            vectors,
            up_weight,
            qkv_weight,
        ],
    )
    joined = call(
        join_kernel,
        ((NROW, ROWS + 8, WIDE), bf16),
        [],
        [order, prefix, tails],
        [pltpu.VMEM((ROWS, PACK), f32)],
    )
    joined = exchange(joined, "row")
    partial = call(
        out_kernel,
        ((NCOL, ROWS, BLOCK), bf16),
        [],
        [joined, out_weight, base],
    )
    partial = exchange(partial, "col")
    hidden_one, partial = call(
        up_kernel,
        [((ROWS, BLOCK), f32), ((NROW, ROWS + 8, BLOCK), bf16)],
        [],
        [partial, vectors, up_rows, up_weight],
    )
    partial = exchange(partial, "row")
    hidden_two = call(
        hidden_kernel,
        ((NROW, ROWS, BLOCK), bf16),
        [],
        [partial, vectors],
        [pltpu.VMEM((2, ROWS, 128), f32)],
    )
    hidden_two = exchange(hidden_two, "row")
    partial = call(
        down_kernel, ((NCOL, ROWS, BLOCK), bf16), [], [hidden_two, down_weight, vectors]
    )
    partial = exchange(partial, "col")
    own, partial = call(
        next_kernel,
        [((ROWS, share), bf16), ((NROW, ROWS + ROWS // 2 + 8, 128), bf16)],
        [],
        [partial, hidden_one, vectors, qkv_rows, qkv_weight],
    )
    partial = exchange(partial, "row")
    layer_out, projected_next, score_sum = call(
        final_kernel,
        [((ROWS, share), bf16), ((cont_local, 2, width), bf16), ((2, cont_local), f32)],
        [],
        [partial, vectors, own],
        [pltpu.VMEM((ROWS, width), f32), pltpu.VMEM((ROWS, 128), f32)],
    )
    return (layer_out.reshape(cont_local, 2, share), score_sum.T, projected_next)


def solution(mesh):
    in_specs = (
        P("pages", None, ("row", "col")),
        P("pages", None, None, "col"),
        P("pages", None, "row", "col"),
        P("pages", None, "row", "col"),
        P(),
        P(),
        P(),
        P(),
        P("col", "row"),
        P(("row", "col")),
        P("row"),
        P("row"),
        P("row", "col"),
        P(("col", "row")),
        P("col", "row"),
        P(("row", "col")),
        P("row"),
        P("row"),
        P("row"),
        P("row", "col"),
        P(("col", "row")),
    )
    out_specs = (
        P("pages", None, ("row", "col")),
        P("pages", None),
        P("pages", None, ("col", "row")),
    )
    return jax.shard_map(shards, mesh=mesh, in_specs=in_specs, out_specs=out_specs, check_vma=False)
```
